32 devices in a mesh: ctx: 8 (over z, y), head: 4 (over x, core).
Axes of the slice: x: 2, y: 2, z: 4, core: 2. Of those that a mesh axis runs over, the one named last changes fastest.
Arguments:
- queries: bfloat16 [2048, 4096], P(('ctx', 'head')), may hold values from -6.5 to 6.5
- keys: bfloat16 [2048, 2048], P(('ctx', 'head')), may hold values from -6.5 to 6.5
- values: bfloat16 [2048, 2048], P(('ctx', 'head')), may hold values from -6 to 6
- grad_out: bfloat16 [2048, 4096], P(('ctx', 'head')), may hold values from -6 to 6
- segments: int32 [2048], P('ctx'), may hold values from 0 to 3, never falling along the last dimension, each value on 1 to 1024 neighbouring positions
Outputs:
- attended: bfloat16 [2048, 4096], P(('ctx', 'head'))
- grad_queries: bfloat16 [2048, 4096], P(('ctx', 'head'))
- grad_keys: bfloat16 [2048, 2048], P(('ctx', 'head'))
- grad_values: bfloat16 [2048, 2048], P(('ctx', 'head'))
The draws below stay inside these ranges and needn't reach their ends.
Inputs may be any that keep to these rules, and one draw needn't show every extreme that they name: `segments`: document numbers never fall along the sequence; each document holds 1 to 1024 tokens.
All inputs are finite; a program needn't handle non-finite values.
Results may differ from the reference program's by a relative error of at most 0.019.
Values may be sent and summed in bfloat16 or wider, within the bound.
No kernel may reach another device: no remote copies, remote signals or barrier semaphores. Data moves between devices by JAX's collectives and lax.ppermute only.
A program may use at most 64 MiB of HBM per device.

```python
import math
import jax
import jax.numpy as jnp
import numpy as np
from jax import lax

QHEADS = 32
KVHEADS = 16
HEAD_DIM = 128
WINDOW = 1024
TOKENS = 2048
DOCS = 4
DOC_MOST = 1024


def base_rows(key, width, salt):
    sample_key = jax.random.fold_in(jax.random.fold_in(key, salt), 0)
    return jnp.clip(jax.random.normal(sample_key, (TOKENS, width), jnp.float32), -6.0, 6.0)


def draw_queries(key, part):
    drawn = base_rows(key, QHEADS * HEAD_DIM, 11)
    return drawn.astype(jnp.bfloat16)


def draw_keys(key, part):
    drawn = base_rows(key, KVHEADS * HEAD_DIM, 23)
    return drawn.astype(jnp.bfloat16)


def block_scale(stream_key, dims, cuts, least, high):
    level = 1.0
    for dim, blocks in cuts:
        steps = jax.random.uniform(jax.random.fold_in(jax.random.fold_in(stream_key, 6), dim), (blocks,), jnp.float32, least / len(cuts), high / len(cuts))
        level = level * jnp.repeat(jnp.exp(steps), dims[dim] // blocks).reshape((-1,) + (1,) * (len(dims) - 1 - dim))
    return level


def split_up(count, total, reach, skew):
    loads = [(1 << 20) // math.isqrt(rank ** skew) + 1 for rank in range(2, count + 1)]
    spare, counts = total - reach - (count - 1), [1] * (count - 1)
    while spare > 0:
        candidates = [i for i in range(count - 1) if counts[i] < reach]
        whole, left = sum([loads[i] for i in candidates]), spare
        for i in candidates:
            more = min(reach - counts[i], max(1, left * loads[i] // whole), spare)
            counts[i] = counts[i] + more
            spare = spare - more
    return np.array([reach] + counts)


def ragged_sizes(key, count, total, bound, slope):
    if count == 2:
        one = jax.random.randint(key, (), max(1, total - bound), min(bound, total - 1) + 1)
        return jnp.stack([one, total - one])
    tallies = jnp.asarray(split_up(count, total, bound, slope), jnp.int32)
    twos = (count - 1) // 2
    source_of, receiver = tallies[1:1 + 2 * twos:2], tallies[2:2 + 2 * twos:2]
    slack = jnp.minimum(source_of - 1, bound - receiver)
    passed = jax.random.randint(jax.random.fold_in(key, 1), (twos,), 0, 1 << 20) % (slack + 1)
    tallies = tallies.at[1:1 + 2 * twos:2].set(source_of - passed).at[2:2 + 2 * twos:2].set(receiver + passed)
    return tallies[jax.random.permutation(jax.random.fold_in(key, 2), count)]


def noise(stream_key, extent, deviation, most, shards=(), kind=jnp.bfloat16):
    values = jax.random.normal(stream_key, extent, jnp.float32) * deviation
    if len(shards) > 0:
        values = block_scale(stream_key, extent, shards, -0.22, 0.18) * values
    return jnp.clip(values, min=-most, max=most).astype(kind)


def setup_inputs(seed: int = 0) -> dict:
    splits = jax.random.split(jax.random.key(seed), 6)
    queries = draw_queries(jax.random.fold_in(splits[5], 71), 0)
    keys = draw_keys(jax.random.fold_in(splits[5], 71), 0)
    values = noise(splits[2], (TOKENS, KVHEADS * HEAD_DIM), 1.0, 6.0, ((0, 32),))
    grad_out = noise(splits[3], (TOKENS, QHEADS * HEAD_DIM), 1.0, 6.0, ((0, 32),))
    segments = jnp.searchsorted(jnp.cumsum(ragged_sizes(splits[4], DOCS, TOKENS, DOC_MOST, 2)), jnp.arange(TOKENS), side="right").astype(jnp.int32)
    return dict(queries=queries, keys=keys, values=values, grad_out=grad_out, segments=segments)


ATTN_SCALE = 168.0 ** -0.5
HIGHEST = lax.Precision.HIGHEST


def window_mask(query_ids, key_ids, query_pos, key_pos):
    distance = query_pos[:, None] - key_pos[None, :]
    return (query_ids[:, None] == key_ids[None, :]) & (distance >= 0) & (distance < WINDOW)


def to_low(array):
    return lax.optimization_barrier(array.astype(jnp.bfloat16)).astype(jnp.float32)


def reference(queries, keys, values, grad_out, segments):
    per_group = QHEADS // KVHEADS
    block_count = TOKENS // WINDOW
    query_heads = queries.reshape(TOKENS, KVHEADS, per_group, HEAD_DIM)
    grad_heads = grad_out.reshape(TOKENS, KVHEADS, per_group, HEAD_DIM)
    key_heads = keys.reshape(TOKENS, KVHEADS, HEAD_DIM)
    value_heads = values.reshape(TOKENS, KVHEADS, HEAD_DIM)
    blank_pairs = jnp.zeros((WINDOW, KVHEADS, HEAD_DIM), jnp.bfloat16)
    padded_keys = jnp.concatenate((blank_pairs, key_heads), 0)
    padded_values = jnp.concatenate((blank_pairs, value_heads), 0)
    blank_ids = jnp.full((WINDOW,), -1, jnp.int32)
    padded_ids = jnp.concatenate((blank_ids, segments), 0)
    positions = jnp.arange(WINDOW, dtype=jnp.int32)
    key_span = jnp.arange(2 * WINDOW, dtype=jnp.int32)

    def forward_block(block_index):
        start = (block_index * WINDOW).astype(jnp.int32)
        block_queries = lax.dynamic_slice_in_dim(query_heads, start, WINDOW, 0).astype(jnp.float32)
        block_grads = lax.dynamic_slice_in_dim(grad_heads, start, WINDOW, 0).astype(jnp.float32)
        near_keys = lax.dynamic_slice_in_dim(padded_keys, start, 2 * WINDOW, 0).astype(jnp.float32)
        near_values = lax.dynamic_slice_in_dim(padded_values, start, 2 * WINDOW, 0).astype(jnp.float32)
        query_ids = lax.dynamic_slice_in_dim(segments, start, WINDOW, 0)
        key_ids = lax.dynamic_slice_in_dim(padded_ids, start, 2 * WINDOW, 0)
        visible = window_mask(query_ids, key_ids, positions + WINDOW, key_span)
        scores = jnp.einsum("agnd,cgd->gnac", block_queries, near_keys, precision=HIGHEST) * ATTN_SCALE
        masked = jnp.where(visible[None, None], scores, -jnp.inf)
        highest = jnp.max(masked, axis=3, keepdims=True)
        weights = jnp.exp(masked - highest)
        totals = jnp.sum(weights, axis=3, keepdims=True)
        probs = weights / totals
        logsum = (highest + jnp.log(totals))[..., 0]
        probs_low = to_low(probs)
        outputs = jnp.einsum("gnac,cgd->agnd", probs_low, near_values, precision=HIGHEST).astype(jnp.bfloat16)
        delta = jnp.sum(outputs.astype(jnp.float32) * block_grads, axis=3)
        prob_grads = jnp.einsum("agnd,cgd->gnac", block_grads, near_values, precision=HIGHEST)
        score_grads = to_low(ATTN_SCALE * probs * (prob_grads - jnp.transpose(delta, (1, 2, 0))[..., None]))
        query_grads = jnp.einsum("gnac,cgd->agnd", score_grads, near_keys, precision=HIGHEST).astype(jnp.bfloat16)
        return outputs, query_grads, logsum, delta

    block_ids = jnp.arange(block_count, dtype=jnp.int32)
    outputs, query_grads, logsum, delta = lax.map(forward_block, block_ids)
    attended = outputs.reshape(TOKENS, QHEADS * HEAD_DIM)
    grad_queries = query_grads.reshape(TOKENS, QHEADS * HEAD_DIM)
    logsum_all = jnp.transpose(logsum, (0, 3, 1, 2)).reshape(TOKENS, KVHEADS, per_group)
    delta_all = delta.reshape(TOKENS, KVHEADS, per_group)

    blank_queries = jnp.zeros((WINDOW, KVHEADS, per_group, HEAD_DIM), jnp.bfloat16)
    later_queries = jnp.concatenate((query_heads, blank_queries), 0)
    later_grads = jnp.concatenate((grad_heads, blank_queries), 0)
    later_ids = jnp.concatenate((segments, blank_ids), 0)
    blank_stats = jnp.zeros((WINDOW, KVHEADS, per_group), jnp.float32)
    later_logsum = jnp.concatenate((logsum_all, blank_stats), 0)
    later_delta = jnp.concatenate((delta_all, blank_stats), 0)

    def backward_block(block_index):
        start = (block_index * WINDOW).astype(jnp.int32)
        own_keys = lax.dynamic_slice_in_dim(key_heads, start, WINDOW, 0).astype(jnp.float32)
        own_values = lax.dynamic_slice_in_dim(value_heads, start, WINDOW, 0).astype(jnp.float32)
        block_queries = lax.dynamic_slice_in_dim(later_queries, start, 2 * WINDOW, 0).astype(jnp.float32)
        block_grads = lax.dynamic_slice_in_dim(later_grads, start, 2 * WINDOW, 0).astype(jnp.float32)
        key_ids = lax.dynamic_slice_in_dim(segments, start, WINDOW, 0)
        query_ids = lax.dynamic_slice_in_dim(later_ids, start, 2 * WINDOW, 0)
        visible = window_mask(query_ids, key_ids, key_span, positions)
        scores = jnp.einsum("agnd,cgd->gnac", block_queries, own_keys, precision=HIGHEST) * ATTN_SCALE
        block_logsum = jnp.transpose(lax.dynamic_slice_in_dim(later_logsum, start, 2 * WINDOW, 0), (1, 2, 0))
        block_delta = jnp.transpose(lax.dynamic_slice_in_dim(later_delta, start, 2 * WINDOW, 0), (1, 2, 0))
        probs = jnp.where(visible[None, None], jnp.exp(scores - block_logsum[..., None]), 0.0)
        probs_low = to_low(probs)
        value_grads = jnp.einsum("gnac,agnd->cgd", probs_low, block_grads, precision=HIGHEST).astype(jnp.bfloat16)
        prob_grads = jnp.einsum("agnd,cgd->gnac", block_grads, own_values, precision=HIGHEST)
        score_grads = to_low(ATTN_SCALE * probs * (prob_grads - block_delta[..., None]))
        key_grads = jnp.einsum("gnac,agnd->cgd", score_grads, block_queries, precision=HIGHEST).astype(jnp.bfloat16)
        return key_grads, value_grads

    key_grads, value_grads = lax.map(backward_block, block_ids)
    grad_keys = key_grads.reshape(TOKENS, KVHEADS * HEAD_DIM)
    grad_values = value_grads.reshape(TOKENS, KVHEADS * HEAD_DIM)
    return attended, grad_queries, grad_keys, grad_values
```

```python
import jax
import jax.numpy as jnp
import numpy as np
from jax import lax
from jax.experimental import pallas as pl
from jax.experimental.pallas import tpu as pltpu
from jax.sharding import Mesh, PartitionSpec as P

QHEADS = 32
KVHEADS = 16
HEAD_DIM = 128
WINDOW = 1024
PER_GROUP = QHEADS // KVHEADS

ATTN_SCALE = 168.0 ** (-0.5)
EXP_SCALE = ATTN_SCALE * 1.4426950408889634
HIDDEN = -1e30
TILE = 256
F32 = jnp.float32
BF16 = jnp.bfloat16
WHOLE = pl.BlockSpec(memory_space=pltpu.VMEM)
SCALARS = pl.BlockSpec(memory_space=pltpu.SMEM)


def dot(a, b, contract):
    return lax.dot_general(a, b, ((contract[0], contract[1]), ((), ())), preferred_element_type=F32)


def pack_kernel(groups, heads, q_ref, g_ref, k_ref, v_ref, out_ref):
    qw = heads * PER_GROUP * HEAD_DIM
    kw = heads * HEAD_DIM
    for j in range(groups):
        out_ref[j, :, 0:qw] = q_ref[:, j * qw : (j + 1) * qw]
        out_ref[j, :, qw : 2 * qw] = g_ref[:, j * qw : (j + 1) * qw]
        out_ref[j, :, 2 * qw : 2 * qw + kw] = k_ref[:, j * kw : (j + 1) * kw]
        out_ref[j, :, 2 * qw + kw :] = v_ref[:, j * kw : (j + 1) * kw]


def unpack_kernel(groups, heads, count, *refs):
    ins, (o_ref, dq_ref, dk_ref, dv_ref) = refs[:count], refs[count:]
    main, side = ins[0], ins[-1]
    qw = heads * PER_GROUP * HEAD_DIM
    kw = heads * HEAD_DIM
    base = 2 * qw if count == 1 else 0
    for j in range(groups):
        o_ref[:, j * qw : (j + 1) * qw] = main[j, :, 0:qw]
        dq_ref[:, j * qw : (j + 1) * qw] = main[j, :, qw : 2 * qw]
        dk_ref[:, j * kw : (j + 1) * kw] = side[j, :, base : base + kw]
        dv_ref[:, j * kw : (j + 1) * kw] = side[j, :, base + kw : base + 2 * kw]


def attention_kernel(rows, prev, split, *refs):
    if prev:
        first_ref, low_ref, x_ref, before_ref, *rest = refs
    else:
        first_ref, low_ref, x_ref, *rest = refs
        before_ref = None
    if split:
        out_ref, own_ref, back_ref, *scratch = rest
    else:
        out_ref, *scratch = rest
        own_ref = back_ref = None
    k_sc, v_sc, kt_sc, vt_sc, s_sc, dk_sc, dv_sc = scratch
    d = HEAD_DIM
    qw = PER_GROUP * d
    q_tiles = rows // TILE
    prev_tiles = prev // TILE
    wide = PER_GROUP * TILE

    for t in range(prev_tiles + q_tiles):
        if t < prev_tiles:
            k = before_ref[t * TILE : (t + 1) * TILE, 0:d]
            v = before_ref[t * TILE : (t + 1) * TILE, d : 2 * d]
        else:
            r = (t - prev_tiles) * TILE
            k = x_ref[r : r + TILE, 2 * qw : 2 * qw + d]
            v = x_ref[r : r + TILE, 2 * qw + d : 2 * qw + 2 * d]
        k_sc[t] = k
        v_sc[t] = v
        kt_sc[t] = k.T
        vt_sc[t] = v.T
        dk_sc[t] = jnp.zeros((TILE, d), F32)
        dv_sc[t] = jnp.zeros((TILE, d), F32)

    lanes = lax.broadcasted_iota(jnp.int32, (1, wide), 1) % TILE
    key_rows = lax.broadcasted_iota(jnp.int32, (TILE, wide), 0)

    def one_tile(i, carry):
        r = pl.multiple_of(i * TILE, TILE)
        q = jnp.concatenate([x_ref[pl.ds(r, TILE), n * d : (n + 1) * d] for n in range(PER_GROUP)], 0)
        g = jnp.concatenate(
            [x_ref[pl.ds(r, TILE), qw + n * d : qw + (n + 1) * d] for n in range(PER_GROUP)], 0
        )
        low = jnp.concatenate([low_ref[pl.ds(i, 1), :]] * PER_GROUP, 1)
        high = lanes + r
        first = first_ref[i]
        last = i + prev_tiles + 1

        def scores(t, top):
            s = dot(k_sc[t], q, ((1,), (1,)))
            pos = key_rows + (t - prev_tiles) * TILE
            s = jnp.where((pos >= low) & (pos <= high), s, HIDDEN)
            s_sc[t] = s
            return jnp.maximum(top, jnp.max(s, axis=0, keepdims=True))

        top = lax.fori_loop(first, last, scores, jnp.full((1, wide), HIDDEN, F32))

        def forward(t, carry):
            total, acc = carry
            e = jnp.exp2((s_sc[t] - top) * EXP_SCALE)
            s_sc[t] = e
            total = total + jnp.sum(e, axis=0, keepdims=True)
            acc = acc + dot(vt_sc[t], e.astype(BF16), ((1,), (0,)))
            return total, acc

        total, acc = lax.fori_loop(
            first, last, forward, (jnp.zeros((1, wide), F32), jnp.zeros((d, wide), F32))
        )
        inverse = 1.0 / total
        attended = (acc * inverse).astype(BF16)
        delta = jnp.sum(attended.astype(F32) * g.T.astype(F32), axis=0, keepdims=True)
        weight = inverse * ATTN_SCALE

        def backward(t, dq):
            e = s_sc[t]
            dp = dot(v_sc[t], g, ((1,), (1,)))
            p = (e * inverse).astype(BF16)
            ds = (e * weight * (dp - delta)).astype(BF16)
            dk_sc[t] += dot(ds, q, ((1,), (0,)))
            dv_sc[t] += dot(p, g, ((1,), (0,)))
            return dq + dot(kt_sc[t], ds, ((1,), (0,)))

        dq = lax.fori_loop(first, last, backward, jnp.zeros((d, wide), F32))
        attended = attended.T
        dq = dq.T.astype(BF16)
        for n in range(PER_GROUP):
            out_ref[pl.ds(r, TILE), n * d : (n + 1) * d] = attended[n * TILE : (n + 1) * TILE]
            out_ref[pl.ds(r, TILE), qw + n * d : qw + (n + 1) * d] = dq[n * TILE : (n + 1) * TILE]
        return carry

    lax.fori_loop(0, q_tiles, one_tile, 0)

    for t in range(prev_tiles + q_tiles):
        if t < prev_tiles:
            back_ref[t * TILE : (t + 1) * TILE, 0:d] = dk_sc[t].astype(BF16)
            back_ref[t * TILE : (t + 1) * TILE, d : 2 * d] = dv_sc[t].astype(BF16)
            continue
        r = (t - prev_tiles) * TILE
        if split:
            own_ref[r : r + TILE, 0:d] = dk_sc[t]
            own_ref[r : r + TILE, d : 2 * d] = dv_sc[t]
        else:
            out_ref[r : r + TILE, 2 * qw : 2 * qw + d] = dk_sc[t].astype(BF16)
            out_ref[r : r + TILE, 2 * qw + d : 2 * qw + 2 * d] = dv_sc[t].astype(BF16)


def attend(first, low, x, before):
    rows = x.shape[0]
    prev = 0 if before is None else before.shape[0]
    split = prev > 0
    d = HEAD_DIM
    qw = PER_GROUP * d
    tiles = (rows + prev) // TILE
    if split:
        out_shape = (
            jax.ShapeDtypeStruct((rows, 2 * qw), BF16),
            jax.ShapeDtypeStruct((rows, 2 * d), F32),
            jax.ShapeDtypeStruct((prev, 2 * d), BF16),
        )
        operands = (first, low, x, before)
    else:
        out_shape = (jax.ShapeDtypeStruct((rows, 2 * qw + 2 * d), BF16),)
        operands = (first, low, x)

    def kernel(*refs):
        attention_kernel(rows, prev, split, *refs)

    return pl.pallas_call(
        kernel,
        name=f"attention_{prev}",
        out_shape=out_shape,
        in_specs=[SCALARS] + [WHOLE] * (len(operands) - 1),
        out_specs=[WHOLE] * len(out_shape),
        scratch_shapes=[
            pltpu.VMEM((tiles, TILE, d), BF16),
            pltpu.VMEM((tiles, TILE, d), BF16),
            pltpu.VMEM((tiles, d, TILE), BF16),
            pltpu.VMEM((tiles, d, TILE), BF16),
            pltpu.VMEM((tiles, TILE, PER_GROUP * TILE), F32),
            pltpu.VMEM((tiles, TILE, d), F32),
            pltpu.VMEM((tiles, TILE, d), F32),
        ],
        compiler_params=pltpu.CompilerParams(vmem_limit_bytes=40 << 20),
    )(*operands)


def body(queries, keys, values, grad_out, segments):
    d = HEAD_DIM
    qw = PER_GROUP * d
    blocks, subs, heads = (lax.axis_size(a) for a in ("block", "sub", "head"))
    groups = subs * heads
    local = queries.shape[0]
    run = segments.shape[0]
    rows = run * subs
    assert groups == KVHEADS and rows == WINDOW and run == TILE
    q_tiles = rows // TILE

    packed = pl.pallas_call(
        lambda *refs: pack_kernel(groups, 1, *refs),
        name="pack",
        out_shape=jax.ShapeDtypeStruct((groups, local, 2 * qw + 2 * d), BF16),
        in_specs=[WHOLE] * 4,
        out_specs=WHOLE,
    )(queries, grad_out, keys, values)
    x = lax.all_to_all(packed, ("sub", "head"), 0, 0, tiled=True).reshape(rows, 2 * qw + 2 * d)

    runs = blocks * subs
    block = lax.axis_index("block")
    place = block * subs + lax.axis_index("sub")
    ids = jnp.where(jnp.arange(runs, dtype=jnp.int32)[:, None] == place, segments[None, :], 0)
    step = 1
    while step < runs:
        if step < subs:
            other = lax.ppermute(ids, "sub", [(i, i ^ step) for i in range(subs)])
        else:
            hop = step // subs
            other = lax.ppermute(ids, "block", [(i, i ^ hop) for i in range(blocks)])
        ids = jnp.maximum(ids, other)
        step *= 2

    total = runs * run
    flat = ids.reshape(total)
    own = lax.dynamic_slice_in_dim(flat, block * rows, rows, 0)
    start = jnp.sum((flat[None, :] < own[:, None]).astype(jnp.int32), axis=1)
    position = block * rows + jnp.arange(rows, dtype=jnp.int32)
    low = jnp.maximum(start, position - (WINDOW - 1)) - block * rows
    low = low.reshape(q_tiles, TILE)
    first = low[:, 0] // TILE
    needed = jnp.int32(0)
    if blocks > 1:
        ends = ids[:, run - 1].reshape(blocks, subs)[: blocks - 1]
        starts = ids[:, 0].reshape(blocks, subs)[1:, :1]
        needed = jnp.max(jnp.sum((ends == starts).astype(jnp.int32), axis=1))

    def swap(value):
        return lax.all_to_all(value, ("sub", "head"), 0, 0, tiled=True)

    def unpack(*parts):
        return pl.pallas_call(
            lambda *refs: unpack_kernel(groups, 1, len(parts), *refs),
            name="unpack",
            out_shape=(
                jax.ShapeDtypeStruct(queries.shape, BF16),
                jax.ShapeDtypeStruct(queries.shape, BF16),
                jax.ShapeDtypeStruct(keys.shape, BF16),
                jax.ShapeDtypeStruct(keys.shape, BF16),
            ),
            in_specs=[WHOLE] * len(parts),
            out_specs=[WHOLE] * 4,
        )(*parts)

    def alone(x, low, first):
        (out,) = attend(first, low, x, None)
        return unpack(swap(out.reshape(groups, local, 2 * qw + 2 * d)))

    def reaching(count):
        def branch(x, low, first):
            prev = count * run
            tail = x[rows - prev :, 2 * qw :]
            before = lax.ppermute(tail, "block", [(i, i + 1) for i in range(blocks - 1)])
            out, kv, back = attend(first + prev // TILE, low, x, before)
            main = swap(out.reshape(groups, local, 2 * qw))
            late = lax.ppermute(back, "block", [(i + 1, i) for i in range(blocks - 1)])
            kv = kv + jnp.pad(late.astype(F32), ((rows - prev, 0), (0, 0)))
            side = swap(kv.astype(BF16).reshape(groups, local, 2 * d))
            return unpack(main, side)

        return branch

    if blocks == 1:
        return alone(x, low, first)
    counts = tuple(range(1, subs + 1))
    return lax.switch(needed, [alone] + [reaching(c) for c in counts], x, low, first)


def solution(mesh):
    shape = dict(mesh.shape)
    devices = np.asarray(mesh.devices)

    def program(queries, keys, values, grad_out, segments):
        run = segments.shape[0] // shape["ctx"]
        subs = WINDOW // run
        fine = Mesh(
            devices.reshape(shape["ctx"] // subs, subs, shape["head"]), ("block", "sub", "head")
        )
        spread = P(("block", "sub", "head"), None)
        return jax.shard_map(
            body,
            mesh=fine,
            in_specs=(spread, spread, spread, spread, P(("block", "sub"))),
            out_specs=(spread, spread, spread, spread),
            check_vma=False,
        )(queries, keys, values, grad_out, segments)

    return program
```

```python
import jax
import jax.numpy as jnp
import numpy as np
from jax import lax
from jax.experimental import pallas as pl
from jax.experimental.pallas import tpu as pltpu
from jax.sharding import Mesh, PartitionSpec as P


QHEADS = 32
KVHEADS = 16
HEAD_DIM = 128
WINDOW = 1024
PER_GROUP = QHEADS // KVHEADS

ATTN_SCALE = 168.0 ** (-0.5)
EXP_SCALE = ATTN_SCALE * 1.4426950408889634
HIDDEN = -1e30
TILE = 256
F32 = jnp.float32
BF16 = jnp.bfloat16
WHOLE = pl.BlockSpec(memory_space=pltpu.VMEM)
SCALARS = pl.BlockSpec(memory_space=pltpu.SMEM)


def dot(a, b, contract):
    return lax.dot_general(a, b, ((contract[0], contract[1]), ((), ())), preferred_element_type=F32)


def pack_kernel(groups, heads, q_ref, g_ref, k_ref, v_ref, out_ref):
    qw = heads * PER_GROUP * HEAD_DIM
    kw = heads * HEAD_DIM
    for j in range(groups):
        out_ref[j, :, 0:qw] = q_ref[:, j * qw : (j + 1) * qw]
        out_ref[j, :, qw : 2 * qw] = g_ref[:, j * qw : (j + 1) * qw]
        out_ref[j, :, 2 * qw : 2 * qw + kw] = k_ref[:, j * kw : (j + 1) * kw]
        out_ref[j, :, 2 * qw + kw :] = v_ref[:, j * kw : (j + 1) * kw]


def unpack_kernel(groups, heads, count, *refs):
    ins, (o_ref, dq_ref, dk_ref, dv_ref) = refs[:count], refs[count:]
    main, side = ins[0], ins[-1]
    qw = heads * PER_GROUP * HEAD_DIM
    kw = heads * HEAD_DIM
    base = 2 * qw if count == 1 else 0
    for j in range(groups):
        o_ref[:, j * qw : (j + 1) * qw] = main[j, :, 0:qw]
        dq_ref[:, j * qw : (j + 1) * qw] = main[j, :, qw : 2 * qw]
        dk_ref[:, j * kw : (j + 1) * kw] = side[j, :, base : base + kw]
        dv_ref[:, j * kw : (j + 1) * kw] = side[j, :, base + kw : base + 2 * kw]


def attention_kernel(rows, prev, split, *refs):
    if prev:
        bounds_ref, low_ref, x_ref, before_ref, *rest = refs
    else:
        bounds_ref, low_ref, x_ref, *rest = refs
        before_ref = None
    if split:
        out_ref, own_ref, back_ref, *scratch = rest
    else:
        out_ref, *scratch = rest
        own_ref = back_ref = None
    k_sc, v_sc, kt_sc, vt_sc, s_sc, e_sc, dk_sc, dv_sc, acc_sc, dq_sc = scratch
    d = HEAD_DIM
    qw = PER_GROUP * d
    q_tiles = rows // TILE
    prev_tiles = prev // TILE
    wide = PER_GROUP * TILE

    for t in range(prev_tiles + q_tiles):
        if t < prev_tiles:
            k = before_ref[t * TILE : (t + 1) * TILE, 0:d]
            v = before_ref[t * TILE : (t + 1) * TILE, d : 2 * d]
            dk_sc[t] = jnp.zeros((TILE, d), F32)
            dv_sc[t] = jnp.zeros((TILE, d), F32)
        else:
            r = (t - prev_tiles) * TILE
            k = x_ref[r : r + TILE, 2 * qw : 2 * qw + d]
            v = x_ref[r : r + TILE, 2 * qw + d : 2 * qw + 2 * d]
        k_sc[t] = k
        v_sc[t] = v
        kt_sc[t] = k.T
        vt_sc[t] = v.T

    lanes = lax.broadcasted_iota(jnp.int32, (1, wide), 1) % TILE
    key_rows = lax.broadcasted_iota(jnp.int32, (TILE, wide), 0)

    def one_tile(i, carry):
        r = i * TILE if isinstance(i, int) else pl.multiple_of(i * TILE, TILE)
        q = jnp.concatenate([x_ref[pl.ds(r, TILE), n * d : (n + 1) * d] for n in range(PER_GROUP)], 0)
        g = jnp.concatenate(
            [x_ref[pl.ds(r, TILE), qw + n * d : qw + (n + 1) * d] for n in range(PER_GROUP)], 0
        )
        low = jnp.concatenate([low_ref[pl.ds(i, 1), :]] * PER_GROUP, 1)
        diagonal = i + prev_tiles
        first = jnp.maximum(bounds_ref[i] + prev_tiles, 0)
        middle = jnp.minimum(jnp.maximum(bounds_ref[q_tiles + i] + prev_tiles, first), diagonal)

        def scores(t, top, edge=False, corner=False):
            s = dot(k_sc[t], q, ((1,), (1,)))
            if edge:
                s = jnp.where(key_rows >= low - (t - prev_tiles) * TILE, s, HIDDEN)
            if corner:
                s = jnp.where(key_rows <= lanes, s, HIDDEN)
            s_sc[t] = s
            return jnp.maximum(top, jnp.max(s, axis=0, keepdims=True))

        top = jnp.full((1, wide), HIDDEN, F32)
        if prev:
            top = lax.fori_loop(first, middle, lambda t, c: scores(t, c, edge=True), top)
            top = lax.fori_loop(middle, diagonal, scores, top)
        else:
            for t in range(i):
                top = scores(t, top, edge=True)
        top = scores(diagonal, top, edge=True, corner=True)
        shift = top * EXP_SCALE

        def forward(t, total, start=False):
            e = jnp.exp2(s_sc[t] * EXP_SCALE - shift)
            low_e = e.astype(BF16)
            e_sc[t] = low_e
            part = dot(vt_sc[t], low_e, ((1,), (0,)))
            if start:
                acc_sc[...] = part
            else:
                acc_sc[...] += part
            return total + jnp.sum(e, axis=0, keepdims=True)

        total = forward(diagonal, jnp.zeros((1, wide), F32), start=True)
        if prev:
            total = lax.fori_loop(first, diagonal, forward, total)
        else:
            for t in range(i):
                total = forward(t, total)
        inverse = 1.0 / total
        attended = (acc_sc[...] * inverse).astype(BF16)
        delta = jnp.sum(attended.astype(F32) * g.T.astype(F32), axis=0, keepdims=True)
        down = jnp.broadcast_to(inverse, (d, wide)).T
        gs = (g.astype(F32) * down).astype(BF16)
        qs = (q.astype(F32) * (down * ATTN_SCALE)).astype(BF16)

        def backward(t, carry, start=False):
            e = e_sc[t]
            dp = dot(v_sc[t], g, ((1,), (1,)))
            ds = (e.astype(F32) * (dp - delta)).astype(BF16)
            dk = dot(ds, qs, ((1,), (0,)))
            dv = dot(e, gs, ((1,), (0,)))
            dq = dot(kt_sc[t], ds, ((1,), (0,)))
            if start:
                dk_sc[t] = dk
                dv_sc[t] = dv
                dq_sc[...] = dq
            else:
                dk_sc[t] += dk
                dv_sc[t] += dv
                dq_sc[...] += dq
            return carry

        backward(diagonal, 0, start=True)
        if prev:
            lax.fori_loop(first, diagonal, backward, 0)
        else:
            for t in range(i):
                backward(t, 0)
        attended = attended.T
        dq = (dq_sc[...] * (inverse * ATTN_SCALE)).astype(BF16).T
        for n in range(PER_GROUP):
            out_ref[pl.ds(r, TILE), n * d : (n + 1) * d] = attended[n * TILE : (n + 1) * TILE]
            out_ref[pl.ds(r, TILE), qw + n * d : qw + (n + 1) * d] = dq[n * TILE : (n + 1) * TILE]
        return carry

    if prev:
        lax.fori_loop(0, q_tiles, one_tile, 0)
    else:
        for i in range(q_tiles):
            one_tile(i, 0)

    for t in range(prev_tiles + q_tiles):
        if t < prev_tiles:
            back_ref[t * TILE : (t + 1) * TILE, 0:d] = dk_sc[t].astype(BF16)
            back_ref[t * TILE : (t + 1) * TILE, d : 2 * d] = dv_sc[t].astype(BF16)
            continue
        r = (t - prev_tiles) * TILE
        if split:
            own_ref[r : r + TILE, 0:d] = dk_sc[t]
            own_ref[r : r + TILE, d : 2 * d] = dv_sc[t]
        else:
            out_ref[r : r + TILE, 2 * qw : 2 * qw + d] = dk_sc[t].astype(BF16)
            out_ref[r : r + TILE, 2 * qw + d : 2 * qw + 2 * d] = dv_sc[t].astype(BF16)


def decide_kernel(subs, run, linked, place_ref, *refs):
    count = subs * (2 if linked else 1)
    scalar, vector = refs[:count], refs[count : 2 * count]
    low_ref, bounds_ref, head_sc, tail_sc = refs[2 * count :]
    block, sub = place_ref[0], place_ref[1]
    ahead = subs if linked else 0
    blank = jnp.full((1, run), -1.0, F32)
    rows = [blank] * count
    for n in range(count):
        turn, own = n % subs, n < subs
        slot = (sub ^ turn) + (ahead if own else 0)
        head_sc[slot] = scalar[n][0, 0]
        tail_sc[slot] = scalar[n][0, run - 1]
        part = vector[n][...].astype(F32)
        for p in range(subs):
            at = p + (ahead if own else 0)
            rows[at] = jnp.where((sub ^ turn) == p, part, rows[at])
    ids = jnp.concatenate(rows, 0)
    lane = lax.broadcasted_iota(jnp.int32, (count, run), 1)
    row = lax.broadcasted_iota(jnp.int32, (count, run), 0)
    spot = ((row - ahead) * run + lane).astype(F32)
    turned = pltpu.roll(ids, 1, 1)
    before = jnp.where(lane == 0, jnp.concatenate([blank, turned[: count - 1]], 0), turned)
    opens = (ids != before) | ((lane == 0) & (row == ahead) & (block == 0))
    far = -4.0 * run * count
    start = jnp.where(opens, spot, far)
    step = 1
    while step < run:
        start = jnp.maximum(start, jnp.where(lane >= step, pltpu.roll(start, step, 1), far))
        step *= 2
    best = [jnp.full((1, run), far, F32)]
    for p in range(count - 1):
        ends = jnp.max(start[p : p + 1], axis=1, keepdims=True)
        best.append(jnp.maximum(best[-1], jnp.broadcast_to(ends, (1, run))))
    start = jnp.maximum(start, jnp.concatenate(best, 0))
    low = jnp.maximum(start, spot - (WINDOW - 1))
    low_ref[...] = low[ahead:].astype(jnp.int32)

    after = head_sc[0]

    @pl.when(block == 0)
    def _():
        for p in range(ahead):
            head_sc[p] = -1
            tail_sc[p] = -1

    reach = WINDOW // run
    for i in range(subs):
        first, middle = -ahead, -ahead
        for t in range(count):
            first += (tail_sc[t] < head_sc[ahead + i]).astype(jnp.int32)
            middle += (head_sc[t] < tail_sc[ahead + i]).astype(jnp.int32)
        bounds_ref[i] = jnp.maximum(first, i - reach)
        bounds_ref[subs + i] = jnp.maximum(middle, i + 1 - reach)
    needed = jnp.int32(0)
    for p in range(ahead):
        needed += (tail_sc[p] == head_sc[ahead]).astype(jnp.int32)
    other = jnp.int32(0)
    if linked == 2:
        for p in range(subs):
            other += (tail_sc[ahead + p] == after).astype(jnp.int32)
    bounds_ref[2 * subs] = jnp.where(block == 0, other, needed)


def attend(bounds, low, x, before):
    rows = x.shape[0]
    prev = 0 if before is None else before.shape[0]
    split = prev > 0
    d = HEAD_DIM
    qw = PER_GROUP * d
    tiles = (rows + prev) // TILE
    if split:
        out_shape = (
            jax.ShapeDtypeStruct((rows, 2 * qw), BF16),
            jax.ShapeDtypeStruct((rows, 2 * d), F32),
            jax.ShapeDtypeStruct((prev, 2 * d), BF16),
        )
        operands = (bounds, low, x, before)
    else:
        out_shape = (jax.ShapeDtypeStruct((rows, 2 * qw + 2 * d), BF16),)
        operands = (bounds, low, x)

    def kernel(*refs):
        attention_kernel(rows, prev, split, *refs)

    return pl.pallas_call(
        kernel,
        out_shape=out_shape,
        in_specs=[SCALARS] + [WHOLE] * (len(operands) - 1),
        out_specs=[WHOLE] * len(out_shape),
        scratch_shapes=[
            pltpu.VMEM((tiles, TILE, d), BF16),
            pltpu.VMEM((tiles, TILE, d), BF16),
            pltpu.VMEM((tiles, d, TILE), BF16),
            pltpu.VMEM((tiles, d, TILE), BF16),
            pltpu.VMEM((tiles, TILE, PER_GROUP * TILE), F32),
            pltpu.VMEM((tiles, TILE, PER_GROUP * TILE), BF16),
            pltpu.VMEM((tiles, TILE, d), F32),
            pltpu.VMEM((tiles, TILE, d), F32),
            pltpu.VMEM((d, PER_GROUP * TILE), F32),
            pltpu.VMEM((d, PER_GROUP * TILE), F32),
        ],
        compiler_params=pltpu.CompilerParams(vmem_limit_bytes=40 << 20),
    )(*operands)


def body(queries, keys, values, grad_out, segments):
    d = HEAD_DIM
    qw = PER_GROUP * d
    blocks, subs, heads = (lax.axis_size(a) for a in ("block", "sub", "head"))
    groups = subs * heads
    local = queries.shape[0]
    run = segments.shape[0]
    rows = run * subs
    assert groups == KVHEADS and rows == WINDOW and run == TILE

    packed = pl.pallas_call(
        lambda *refs: pack_kernel(groups, 1, *refs),
        name="pack",
        out_shape=jax.ShapeDtypeStruct((groups, local, 2 * qw + 2 * d), BF16),
        in_specs=[WHOLE] * 4,
        out_specs=WHOLE,
    )(queries, grad_out, keys, values)
    x = lax.all_to_all(packed, ("sub", "head"), 0, 0, tiled=True).reshape(rows, 2 * qw + 2 * d)

    block = lax.axis_index("block")
    sub = lax.axis_index("sub")
    both = ("block", "sub")
    line = segments.reshape(1, run)

    def turned_ids(back):
        parts = []
        for turn in range(subs):
            route = [
                (((b - back) % blocks) * subs + (s ^ turn), b * subs + s)
                for b in range(blocks)
                for s in range(subs)
            ]
            parts.append(lax.ppermute(line, both, route) if back or turn else line)
        return parts

    linked = 0 if blocks == 1 else 2 if blocks == 2 else 1
    parts = turned_ids(0) + (turned_ids(1) if linked else [])
    low, bounds = pl.pallas_call(
        lambda *refs: decide_kernel(subs, run, linked, *refs),
        name="decide",
        out_shape=(
            jax.ShapeDtypeStruct((subs, run), jnp.int32),
            jax.ShapeDtypeStruct((2 * subs + 1,), jnp.int32),
        ),
        in_specs=[SCALARS] * (1 + len(parts)) + [WHOLE] * len(parts),
        out_specs=[WHOLE, SCALARS],
        scratch_shapes=[pltpu.SMEM((2 * subs,), jnp.int32), pltpu.SMEM((2 * subs,), jnp.int32)],
    )(jnp.stack([block, sub]), *parts, *parts)
    needed = bounds[2 * subs]
    if blocks > 2:
        step = 1
        while step < blocks:
            turned = lax.ppermute(needed, "block", [(i, (i + step) % blocks) for i in range(blocks)])
            needed = jnp.maximum(needed, turned)
            step *= 2

    def swap(value):
        return lax.all_to_all(value, ("sub", "head"), 0, 0, tiled=True)

    def unpack(*parts):
        return pl.pallas_call(
            lambda *refs: unpack_kernel(groups, 1, len(parts), *refs),
            name="unpack",
            out_shape=(
                jax.ShapeDtypeStruct(queries.shape, BF16),
                jax.ShapeDtypeStruct(queries.shape, BF16),
                jax.ShapeDtypeStruct(keys.shape, BF16),
                jax.ShapeDtypeStruct(keys.shape, BF16),
            ),
            in_specs=[WHOLE] * len(parts),
            out_specs=[WHOLE] * 4,
        )(*parts)

    def alone(x, low, bounds):
        (out,) = attend(bounds, low, x, None)
        return unpack(swap(out.reshape(groups, local, 2 * qw + 2 * d)))

    def reaching(count):
        def branch(x, low, bounds):
            prev = count * run
            tail = x[rows - prev :, 2 * qw :]
            before = lax.ppermute(tail, "block", [(i, i + 1) for i in range(blocks - 1)])
            out, kv, back = attend(bounds, low, x, before)
            main = swap(out.reshape(groups, local, 2 * qw))
            late = lax.ppermute(back, "block", [(i + 1, i) for i in range(blocks - 1)])
            kv = kv + jnp.pad(late.astype(F32), ((rows - prev, 0), (0, 0)))
            side = swap(kv.astype(BF16).reshape(groups, local, 2 * d))
            return unpack(main, side)

        return branch

    if blocks == 1:
        return alone(x, low, bounds)
    counts = tuple(range(1, subs + 1))
    return lax.switch(needed, [alone] + [reaching(c) for c in counts], x, low, bounds)


def solution(mesh):
    shape = dict(mesh.shape)
    devices = np.asarray(mesh.devices)

    def program(queries, keys, values, grad_out, segments):
        run = segments.shape[0] // shape["ctx"]
        subs = WINDOW // run
        fine = Mesh(
            devices.reshape(shape["ctx"] // subs, subs, shape["head"]), ("block", "sub", "head")
        )
        spread = P(("block", "sub", "head"), None)
        return jax.shard_map(
            body,
            mesh=fine,
            in_specs=(spread, spread, spread, spread, P(("block", "sub"))),
            out_specs=(spread, spread, spread, spread),
            check_vma=False,
        )(queries, keys, values, grad_out, segments)

    return program
```

```python
import jax
import jax.numpy as jnp
import numpy as np
from jax import lax
from jax.experimental import pallas as pl
from jax.experimental.pallas import tpu as pltpu
from jax.sharding import Mesh, PartitionSpec as P


QHEADS = 32
KVHEADS = 16
HEAD_DIM = 128
WINDOW = 1024
PER_GROUP = QHEADS // KVHEADS

ATTN_SCALE = 168.0 ** (-0.5)
EXP_SCALE = ATTN_SCALE * 1.4426950408889634
HIDDEN = -1e30
TOGETHER = 0
TILE = 256
F32 = jnp.float32
BF16 = jnp.bfloat16
WHOLE = pl.BlockSpec(memory_space=pltpu.VMEM)
ANYWHERE = pl.BlockSpec(memory_space=pl.ANY)
SCALARS = pl.BlockSpec(memory_space=pltpu.SMEM)


def dot(a, b, contract):
    return lax.dot_general(a, b, ((contract[0], contract[1]), ((), ())), preferred_element_type=F32)


def pack_kernel(groups, q_ref, g_ref, k_ref, v_ref, out_ref, q_sc, g_sc, k_sc, v_sc, hold, in_sem, out_sem):
    qw = PER_GROUP * HEAD_DIM
    kw = HEAD_DIM
    half = groups // 2
    pairs = ((q_ref, q_sc, qw, 0), (g_ref, g_sc, qw, qw), (k_ref, k_sc, kw, 2 * qw), (v_ref, v_sc, kw, 2 * qw + kw))

    def fetch(part):
        return [
            pltpu.make_async_copy(
                ref.at[:, part * half * w : (part + 1) * half * w],
                sc.at[:, part * half * w : (part + 1) * half * w],
                in_sem.at[part, n],
            )
            for n, (ref, sc, w, at) in enumerate(pairs)
        ]

    def emit(j):
        return pltpu.make_async_copy(hold.at[j], out_ref.at[j], out_sem.at[j])

    for part in range(2):
        for copy in fetch(part):
            copy.start()
    for part in range(2):
        for copy in fetch(part):
            copy.wait()
        for j in range(part * half, (part + 1) * half):
            for ref, sc, w, at in pairs:
                hold[j, :, at : at + w] = sc[:, j * w : (j + 1) * w]
            emit(j).start()
    for j in range(groups):
        emit(j).wait()


def unpack_kernel(groups, count, *refs):
    ins, (o_ref, dq_ref, dk_ref, dv_ref) = refs[:count], refs[count:]
    main, side = ins[0], ins[-1]
    qw = PER_GROUP * HEAD_DIM
    kw = HEAD_DIM
    base = 2 * qw if count == 1 else 0
    for j in range(groups):
        o_ref[:, j * qw : (j + 1) * qw] = main[j, :, 0:qw]
        dq_ref[:, j * qw : (j + 1) * qw] = main[j, :, qw : 2 * qw]
        dk_ref[:, j * kw : (j + 1) * kw] = side[j, :, base : base + kw]
        dv_ref[:, j * kw : (j + 1) * kw] = side[j, :, base + kw : base + 2 * kw]


def attention_kernel(rows, prev, split, *refs):
    if prev:
        bounds_ref, ids_ref, x_ref, before_ref, *rest = refs
    else:
        bounds_ref, ids_ref, x_ref, *rest = refs
        before_ref = None
    if split:
        out_ref, own_ref, back_ref, *scratch = rest
        kp_sc, vp_sc, ktp_sc, vtp_sc, sp_sc, ep_sc, dkp_sc, dvp_sc, accp_sc, dqp_sc = scratch[7:]
    else:
        out_ref, *scratch = rest
        own_ref = back_ref = None
    kt_sc, vt_sc, s_sc, e_sc, ds_sc, qs_sc, gs_sc = scratch[:7]
    d = HEAD_DIM
    qw = PER_GROUP * d
    q_tiles = rows // TILE
    prev_tiles = prev // TILE
    wide = PER_GROUP * TILE
    key_at, value_at = 2 * qw, 2 * qw + d

    low_all = lowest_keys(ids_ref[...], q_tiles, bounds_ref[2 * q_tiles])
    lanes = lax.broadcasted_iota(jnp.int32, (1, wide), 1) % TILE
    key_rows = lax.broadcasted_iota(jnp.int32, (TILE, wide), 0)
    for t in range(prev_tiles):
        span = slice(t * TILE, (t + 1) * TILE)
        k, v = before_ref[span, 0:d], before_ref[span, d : 2 * d]
        kp_sc[t], vp_sc[t], ktp_sc[t], vtp_sc[t] = k, v, k.T, v.T
        dkp_sc[t] = jnp.zeros((TILE, d), F32)
        dvp_sc[t] = jnp.zeros((TILE, d), F32)

    for i in range(q_tiles):
        span = slice(i * TILE, (i + 1) * TILE)
        cols = slice(i * wide, (i + 1) * wide)
        reach = slice(0, (i + 1) * TILE)
        kt_sc[:, span] = x_ref[span, key_at : key_at + d].T
        vt_sc[:, span] = x_ref[span, value_at : value_at + d].T
        q = jnp.concatenate([x_ref[span, n * d : (n + 1) * d] for n in range(PER_GROUP)], 0)
        g = jnp.concatenate([x_ref[span, qw + n * d : qw + (n + 1) * d] for n in range(PER_GROUP)], 0)
        low = jnp.concatenate([low_all[i : i + 1]] * PER_GROUP, 1)
        first = jnp.maximum(bounds_ref[i] + prev_tiles, 0)

        top = jnp.full((1, wide), HIDDEN, F32)
        for t in range(i + 1):
            at = slice(t * TILE, (t + 1) * TILE)
            s = dot(x_ref[at, key_at : key_at + d], q, ((1,), (1,)))
            s = jnp.where(key_rows >= low - t * TILE, s, HIDDEN)
            if t == i:
                s = jnp.where(key_rows <= lanes, s, HIDDEN)
            s_sc[at, :] = s
            top = jnp.maximum(top, jnp.max(s, axis=0, keepdims=True))

        def scores(t, top):
            s = dot(kp_sc[t], q, ((1,), (1,)))
            s = jnp.where(key_rows >= low - (t - prev_tiles) * TILE, s, HIDDEN)
            sp_sc[t] = s
            return jnp.maximum(top, jnp.max(s, axis=0, keepdims=True))

        if prev:
            top = lax.fori_loop(first, prev_tiles, scores, top)
        shift = top * EXP_SCALE

        total = jnp.zeros((1, wide), F32)
        for t in range(i + 1):
            at = slice(t * TILE, (t + 1) * TILE)
            e = jnp.exp2(s_sc[at, :] * EXP_SCALE - shift)
            e_sc[at, cols] = e.astype(BF16)
            total = total + jnp.sum(e, axis=0, keepdims=True)
        acc = dot(vt_sc[:, reach], e_sc[reach, cols], ((1,), (0,)))

        def forward(t, total):
            e = jnp.exp2(sp_sc[t] * EXP_SCALE - shift)
            small = e.astype(BF16)
            ep_sc[t] = small
            accp_sc[...] += dot(vtp_sc[t], small, ((1,), (0,)))
            return total + jnp.sum(e, axis=0, keepdims=True)

        if prev:
            accp_sc[...] = acc
            total = lax.fori_loop(first, prev_tiles, forward, total)
            acc = accp_sc[...]
        inverse = 1.0 / total
        attended = (acc * inverse).astype(BF16)
        delta = jnp.sum(attended.astype(F32) * g.T.astype(F32), axis=0, keepdims=True)
        down = jnp.broadcast_to(inverse, (d, wide)).T
        gs_sc[cols, :] = (g.astype(F32) * down).astype(BF16)
        qs_sc[cols, :] = (q.astype(F32) * (down * ATTN_SCALE)).astype(BF16)

        for t in range(i + 1):
            at = slice(t * TILE, (t + 1) * TILE)
            dp = dot(x_ref[at, value_at : value_at + d], g, ((1,), (1,)))
            ds_sc[at, cols] = (e_sc[at, cols].astype(F32) * (dp - delta)).astype(BF16)
        dq = dot(kt_sc[:, reach], ds_sc[reach, cols], ((1,), (0,)))

        def backward(t, carry):
            e = ep_sc[t]
            dp = dot(vp_sc[t], g, ((1,), (1,)))
            ds = (e.astype(F32) * (dp - delta)).astype(BF16)
            dkp_sc[t] += dot(ds, qs_sc[cols, :], ((1,), (0,)))
            dvp_sc[t] += dot(e, gs_sc[cols, :], ((1,), (0,)))
            dqp_sc[...] += dot(ktp_sc[t], ds, ((1,), (0,)))
            return carry

        if prev:
            dqp_sc[...] = dq
            lax.fori_loop(first, prev_tiles, backward, 0)
            dq = dqp_sc[...]
        attended = attended.T
        dq = (dq * (inverse * ATTN_SCALE)).astype(BF16).T
        for n in range(PER_GROUP):
            out_ref[span, n * d : (n + 1) * d] = attended[n * TILE : (n + 1) * TILE]
            out_ref[span, qw + n * d : qw + (n + 1) * d] = dq[n * TILE : (n + 1) * TILE]

    for t in range(q_tiles):
        at = slice(t * TILE, (t + 1) * TILE)
        dk = dot(ds_sc[at, t * wide :], qs_sc[t * wide :, :], ((1,), (0,)))
        dv = dot(e_sc[at, t * wide :], gs_sc[t * wide :, :], ((1,), (0,)))
        if split:
            own_ref[at, 0:d] = dk
            own_ref[at, d : 2 * d] = dv
        else:
            out_ref[at, key_at : key_at + d] = dk.astype(BF16)
            out_ref[at, value_at : value_at + d] = dv.astype(BF16)
    for t in range(prev_tiles):
        back_ref[t * TILE : (t + 1) * TILE, 0:d] = dkp_sc[t].astype(BF16)
        back_ref[t * TILE : (t + 1) * TILE, d : 2 * d] = dvp_sc[t].astype(BF16)


def assemble(parts, subs, sub):
    rows = [None] * len(parts)
    for n, part in enumerate(parts):
        turn, base = n % subs, len(parts) - subs if n < subs else 0
        for p in range(subs):
            seen = rows[base + p]
            rows[base + p] = part if seen is None else jnp.where((sub ^ turn) == p, part, seen)
    return jnp.concatenate(rows, 0)


def decide_kernel(subs, run, blocks, place_ref, *refs):
    count = subs * (2 if blocks > 1 else 1)
    ids_ref, bounds_ref, needed_ref = refs[count:]
    block, sub = place_ref[0], place_ref[1]
    ahead = count - subs
    ids = assemble([ref[...] for ref in refs[:count]], subs, sub).astype(F32)
    ids_ref[...] = ids
    heads = jnp.min(ids, axis=1, keepdims=True)
    tails = jnp.max(ids, axis=1, keepdims=True)
    row = lax.broadcasted_iota(jnp.int32, (count, 1), 0)
    if ahead:
        after = jnp.sum((tails[ahead:] == heads[0:1]).astype(F32))
        needed = jnp.sum((tails[:ahead] == heads[ahead : ahead + 1]).astype(F32))
        if blocks > 2:
            after = 0.0
        needed_ref[0] = jnp.where(block == 0, after, needed).astype(jnp.int32)
        absent = (row < ahead) & (block == 0)
        heads = jnp.where(absent, -1.0, heads)
        tails = jnp.where(absent, -1.0, tails)
    else:
        needed_ref[0] = 0
    reach = WINDOW // run
    for i in range(subs):
        first = jnp.sum((tails < heads[ahead + i : ahead + i + 1]).astype(F32)).astype(jnp.int32)
        middle = jnp.sum((heads < tails[ahead + i : ahead + i + 1]).astype(F32)).astype(jnp.int32)
        bounds_ref[i] = jnp.maximum(first - ahead, i - reach)
        bounds_ref[subs + i] = jnp.maximum(middle - ahead, i + 1 - reach)
    bounds_ref[2 * subs] = block


def lowest_keys(ids, subs, block):
    count, run = ids.shape
    ahead = count - subs
    lane = lax.broadcasted_iota(jnp.int32, (count, run), 1)
    row = lax.broadcasted_iota(jnp.int32, (count, run), 0)
    spot = ((row - ahead) * run + lane).astype(F32)
    turned = pltpu.roll(ids, 1, 1)
    lagged = jnp.concatenate([turned[:1], turned[: count - 1]], 0)
    before = jnp.where(lane == 0, lagged, turned)
    opens = (ids != before) | ((lane == 0) & ((row == 0) | ((row == ahead) & (block == 0))))
    far = -4.0 * run * count
    start = jnp.where(opens, spot, far)
    step = 1
    while step < run:
        start = jnp.maximum(start, jnp.where(lane >= step, pltpu.roll(start, step, 1), far))
        step *= 2
    ends = jnp.max(start, axis=1, keepdims=True)
    best = [jnp.full((1, 1), far, F32)]
    for p in range(count - 1):
        best.append(jnp.maximum(best[-1], ends[p : p + 1]))
    start = jnp.maximum(start, jnp.concatenate(best, 0))
    return jnp.maximum(start, spot - (WINDOW - 1))[ahead:].astype(jnp.int32)


def attend(bounds, ids, x, before):
    rows = x.shape[0]
    prev = 0 if before is None else before.shape[0]
    split = prev > 0
    d = HEAD_DIM
    qw = PER_GROUP * d
    wide = PER_GROUP * TILE
    span = PER_GROUP * rows
    tiles = prev // TILE
    own_scratch = [
        pltpu.VMEM((d, rows), BF16),
        pltpu.VMEM((d, rows), BF16),
        pltpu.VMEM((rows, wide), F32),
        pltpu.VMEM((rows, span), BF16),
        pltpu.VMEM((rows, span), BF16),
        pltpu.VMEM((span, d), BF16),
        pltpu.VMEM((span, d), BF16),
    ]
    prev_scratch = [
        pltpu.VMEM((tiles, TILE, d), BF16),
        pltpu.VMEM((tiles, TILE, d), BF16),
        pltpu.VMEM((tiles, d, TILE), BF16),
        pltpu.VMEM((tiles, d, TILE), BF16),
        pltpu.VMEM((tiles, TILE, wide), F32),
        pltpu.VMEM((tiles, TILE, wide), BF16),
        pltpu.VMEM((tiles, TILE, d), F32),
        pltpu.VMEM((tiles, TILE, d), F32),
        pltpu.VMEM((d, wide), F32),
        pltpu.VMEM((d, wide), F32),
    ]
    if split:
        out_shape = (
            jax.ShapeDtypeStruct((rows, 2 * qw), BF16),
            jax.ShapeDtypeStruct((rows, 2 * d), F32),
            jax.ShapeDtypeStruct((prev, 2 * d), BF16),
        )
        operands = (bounds, ids, x, before)
    else:
        out_shape = (jax.ShapeDtypeStruct((rows, 2 * qw + 2 * d), BF16),)
        operands = (bounds, ids, x)

    def kernel(*refs):
        attention_kernel(rows, prev, split, *refs)

    return pl.pallas_call(
        kernel,
        out_shape=out_shape,
        in_specs=[SCALARS] + [WHOLE] * (len(operands) - 1),
        out_specs=[WHOLE] * len(out_shape),
        scratch_shapes=own_scratch + (prev_scratch if split else []),
        compiler_params=pltpu.CompilerParams(vmem_limit_bytes=40 << 20),
    )(*operands)


def body(queries, keys, values, grad_out, segments):
    d = HEAD_DIM
    qw = PER_GROUP * d
    blocks, subs, heads = (lax.axis_size(a) for a in ("block", "sub", "head"))
    groups = subs * heads
    local = queries.shape[0]
    run = segments.shape[0]
    rows = run * subs
    assert groups == KVHEADS and rows == WINDOW and run == TILE

    packed = pl.pallas_call(
        lambda *refs: pack_kernel(groups, *refs),
        name="pack",
        out_shape=jax.ShapeDtypeStruct((groups, local, 2 * qw + 2 * d), BF16),
        in_specs=[ANYWHERE] * 4,
        out_specs=ANYWHERE,
        scratch_shapes=[
            pltpu.VMEM(queries.shape, BF16),
            pltpu.VMEM(queries.shape, BF16),
            pltpu.VMEM(keys.shape, BF16),
            pltpu.VMEM(keys.shape, BF16),
            pltpu.VMEM((groups, local, 2 * qw + 2 * d), BF16),
            pltpu.SemaphoreType.DMA((2, 4)),
            pltpu.SemaphoreType.DMA((groups,)),
        ],
    )(queries, grad_out, keys, values)
    x = lax.all_to_all(packed, ("sub", "head"), 0, 0, tiled=True).reshape(rows, 2 * qw + 2 * d)

    block = lax.axis_index("block")
    sub = lax.axis_index("sub")
    both = ("block", "sub")
    line = segments.reshape(1, run)

    def turned_ids(back):
        parts = []
        for turn in range(subs):
            route = [
                (((b - back) % blocks) * subs + (s ^ turn), b * subs + s)
                for b in range(blocks)
                for s in range(subs)
            ]
            parts.append(lax.ppermute(line, both, route) if back or turn else line)
        return parts

    parts = turned_ids(0) + (turned_ids(1) if blocks > 1 else [])
    ids, bounds, needed = pl.pallas_call(
        lambda *refs: decide_kernel(subs, run, blocks, *refs),
        name="decide",
        out_shape=(
            jax.ShapeDtypeStruct((len(parts), run), F32),
            jax.ShapeDtypeStruct((2 * subs + 1,), jnp.int32),
            jax.ShapeDtypeStruct((1,), jnp.int32),
        ),
        in_specs=[SCALARS] + [WHOLE] * len(parts),
        out_specs=[WHOLE, SCALARS, SCALARS],
        compiler_params=pltpu.CompilerParams(vmem_limit_bytes=1 << 20),
    )(jnp.stack([block, sub]), *parts)
    needed = needed.reshape(())
    if blocks > 2:
        step = 1
        while step < blocks:
            turned = lax.ppermute(needed, "block", [(i, (i + step) % blocks) for i in range(blocks)])
            needed = jnp.maximum(needed, turned)
            step *= 2

    def swap(value):
        return lax.all_to_all(value, ("sub", "head"), 0, 0, tiled=True)

    def unpack(*parts):
        return pl.pallas_call(
            lambda *refs: unpack_kernel(groups, len(parts), *refs),
            name="unpack",
            out_shape=(
                jax.ShapeDtypeStruct(queries.shape, BF16),
                jax.ShapeDtypeStruct(queries.shape, BF16),
                jax.ShapeDtypeStruct(keys.shape, BF16),
                jax.ShapeDtypeStruct(keys.shape, BF16),
            ),
            in_specs=[WHOLE] * len(parts),
            out_specs=[WHOLE] * 4,
            compiler_params=pltpu.CompilerParams(vmem_limit_bytes=8 << 20),
        )(*parts)

    def alone(x, ids, bounds):
        (out,) = attend(bounds, ids, x, None)
        return unpack(swap(out.reshape(groups, local, 2 * qw + 2 * d)))

    onward = [(i, i + 1) for i in range(blocks - 1)]
    backward = [(i + 1, i) for i in range(blocks - 1)]

    def fetch(count):
        def branch(x):
            tail = x[rows - count * run :, 2 * qw :]
            return jnp.pad(lax.ppermute(tail, "block", onward), ((rows - count * run, 0), (0, 0)))

        return branch

    def give(count):
        at = rows - count * run

        def branch(out, kv, back):
            late = lax.ppermute(back[at:], "block", backward)
            kv = (kv + jnp.pad(late.astype(F32), ((at, 0), (0, 0)))).astype(BF16)
            if 2 * count <= TOGETHER:
                both = jnp.concatenate([out, kv], 1)
                return unpack(swap(both.reshape(groups, local, 2 * qw + 2 * d)))
            main = swap(out.reshape(groups, local, 2 * qw))
            side = swap(kv.reshape(groups, local, 2 * d))
            return unpack(main, side)

        return branch

    def reaching(x, ids, bounds):
        case = jnp.clip(needed - 1, 0, subs - 1)
        before = lax.switch(case, [fetch(c + 1) for c in range(subs)], x)
        out, kv, back = attend(bounds, ids, x, before)
        return lax.switch(case, [give(c + 1) for c in range(subs)], out, kv, back)

    if blocks == 1:
        return alone(x, ids, bounds)
    return lax.cond(needed == 0, alone, reaching, x, ids, bounds)


def solution(mesh):
    shape = dict(mesh.shape)
    devices = np.asarray(mesh.devices)

    def program(queries, keys, values, grad_out, segments):
        run = segments.shape[0] // shape["ctx"]
        subs = WINDOW // run
        fine = Mesh(
            devices.reshape(shape["ctx"] // subs, subs, shape["head"]), ("block", "sub", "head")
        )
        spread = P(("block", "sub", "head"), None)
        return jax.shard_map(
            body,
            mesh=fine,
            in_specs=(spread, spread, spread, spread, P(("block", "sub"))),
            out_specs=(spread, spread, spread, spread),
            check_vma=False,
        )(queries, keys, values, grad_out, segments)

    return program
```

```python
import jax
import jax.numpy as jnp
import numpy as np
from jax import lax
from jax.experimental import pallas as pl
from jax.experimental.pallas import tpu as pltpu
from jax.sharding import Mesh, PartitionSpec as P


QHEADS = 32
KVHEADS = 16
HEAD_DIM = 128
WINDOW = 1024
PER_GROUP = QHEADS // KVHEADS

ATTN_SCALE = 168.0 ** (-0.5)
EXP_SCALE = ATTN_SCALE * 1.4426950408889634
HIDDEN = -1e30
TOGETHER = 2
TILE = 256
F32 = jnp.float32
BF16 = jnp.bfloat16
WHOLE = pl.BlockSpec(memory_space=pltpu.VMEM)
ANYWHERE = pl.BlockSpec(memory_space=pl.ANY)
SCALARS = pl.BlockSpec(memory_space=pltpu.SMEM)


def dot(a, b, contract):
    return lax.dot_general(a, b, ((contract[0], contract[1]), ((), ())), preferred_element_type=F32)


def pack_kernel(groups, q_ref, g_ref, k_ref, v_ref, out_ref, q_sc, g_sc, k_sc, v_sc, hold, in_sem, out_sem):
    qw = PER_GROUP * HEAD_DIM
    kw = HEAD_DIM
    half = groups // 2
    pairs = ((q_ref, q_sc, qw, 0), (g_ref, g_sc, qw, qw), (k_ref, k_sc, kw, 2 * qw), (v_ref, v_sc, kw, 2 * qw + kw))

    def fetch(part):
        return [
            pltpu.make_async_copy(
                ref.at[:, part * half * w : (part + 1) * half * w],
                sc.at[:, part * half * w : (part + 1) * half * w],
                in_sem.at[part, n],
            )
            for n, (ref, sc, w, at) in enumerate(pairs)
        ]

    def emit(j):
        return pltpu.make_async_copy(hold.at[j], out_ref.at[j], out_sem.at[j])

    for part in range(2):
        for copy in fetch(part):
            copy.start()
    for part in range(2):
        for copy in fetch(part):
            copy.wait()
        for j in range(part * half, (part + 1) * half):
            for ref, sc, w, at in pairs:
                hold[j, :, at : at + w] = sc[:, j * w : (j + 1) * w]
            emit(j).start()
    for j in range(groups):
        emit(j).wait()


def unpack_kernel(groups, count, *refs):
    ins, (o_ref, dq_ref, dk_ref, dv_ref) = refs[:count], refs[count:]
    main, side = ins[0], ins[-1]
    qw = PER_GROUP * HEAD_DIM
    kw = HEAD_DIM
    base = 2 * qw if count == 1 else 0
    for j in range(groups):
        o_ref[:, j * qw : (j + 1) * qw] = main[j, :, 0:qw]
        dq_ref[:, j * qw : (j + 1) * qw] = main[j, :, qw : 2 * qw]
        dk_ref[:, j * kw : (j + 1) * kw] = side[j, :, base : base + kw]
        dv_ref[:, j * kw : (j + 1) * kw] = side[j, :, base + kw : base + 2 * kw]


def attention_kernel(rows, prev, split, *refs):
    if prev:
        bounds_ref, ids_ref, x_ref, before_ref, *rest = refs
    else:
        bounds_ref, ids_ref, x_ref, *rest = refs
        before_ref = None
    if split:
        out_ref, own_ref, back_ref, *scratch = rest
        kp_sc, vp_sc, ktp_sc, vtp_sc, sp_sc, ep_sc, dkp_sc, dvp_sc, accp_sc, dqp_sc = scratch[9:]
    else:
        out_ref, *scratch = rest
        own_ref = back_ref = None
    kt_sc, vt_sc, s_sc, e_sc, ds_sc, qs_sc, gs_sc, dkt_sc, dvt_sc = scratch[:9]
    d = HEAD_DIM
    qw = PER_GROUP * d
    q_tiles = rows // TILE
    prev_tiles = prev // TILE
    wide = PER_GROUP * TILE
    key_at, value_at = 2 * qw, 2 * qw + d

    low_all = lowest_keys(ids_ref[...], q_tiles, bounds_ref[2 * q_tiles])
    lanes = lax.broadcasted_iota(jnp.int32, (1, wide), 1) % TILE
    key_rows = lax.broadcasted_iota(jnp.int32, (TILE, wide), 0)
    for t in range(prev_tiles):
        span = slice(t * TILE, (t + 1) * TILE)
        k, v = before_ref[span, 0:d], before_ref[span, d : 2 * d]
        kp_sc[t], vp_sc[t], ktp_sc[t], vtp_sc[t] = k, v, k.T, v.T
        dkp_sc[t] = jnp.zeros((d, TILE), F32)
        dvp_sc[t] = jnp.zeros((d, TILE), F32)

    def collect(i, t):
        at = slice(t * TILE, (t + 1) * TILE)
        cols = slice(i * wide, (i + 1) * wide)
        dk = dot(qs_sc[:, cols], ds_sc[at, cols], ((1,), (1,)))
        dv = dot(gs_sc[:, cols], e_sc[at, cols], ((1,), (1,)))
        if t == i:
            dkt_sc[:, at] = dk
            dvt_sc[:, at] = dv
        else:
            dkt_sc[:, at] += dk
            dvt_sc[:, at] += dv

    for i in range(q_tiles):
        span = slice(i * TILE, (i + 1) * TILE)
        cols = slice(i * wide, (i + 1) * wide)
        reach = slice(0, (i + 1) * TILE)
        kt_sc[:, span] = x_ref[span, key_at : key_at + d].T
        vt_sc[0:d, span] = x_ref[span, value_at : value_at + d].T
        vt_sc[d:, span] = jnp.ones((16, TILE), BF16)
        q = jnp.concatenate([x_ref[span, n * d : (n + 1) * d] for n in range(PER_GROUP)], 0)
        g = jnp.concatenate([x_ref[span, qw + n * d : qw + (n + 1) * d] for n in range(PER_GROUP)], 0)
        low = jnp.concatenate([low_all[i : i + 1]] * PER_GROUP, 1)
        first = jnp.maximum(bounds_ref[i] + prev_tiles, 0)

        top = jnp.full((1, wide), HIDDEN, F32)
        for t in range(i + 1):
            at = slice(t * TILE, (t + 1) * TILE)
            s = dot(x_ref[at, key_at : key_at + d], q, ((1,), (1,)))
            s = jnp.where(key_rows >= low - t * TILE, s, HIDDEN)
            if t == i:
                s = jnp.where(key_rows <= lanes, s, HIDDEN)
            s_sc[at, :] = s
            top = jnp.maximum(top, jnp.max(s, axis=0, keepdims=True))

        def scores(t, top):
            s = dot(kp_sc[t], q, ((1,), (1,)))
            s = jnp.where(key_rows >= low - (t - prev_tiles) * TILE, s, HIDDEN)
            sp_sc[t] = s
            return jnp.maximum(top, jnp.max(s, axis=0, keepdims=True))

        if prev:
            top = lax.fori_loop(first, prev_tiles, scores, top)
        shift = top * EXP_SCALE

        for t in range(i + 1):
            at = slice(t * TILE, (t + 1) * TILE)
            e = jnp.exp2(s_sc[at, :] * EXP_SCALE - shift)
            e_sc[at, cols] = e.astype(BF16)
            if t < i:
                collect(i - 1, t)
        acc = dot(vt_sc[:, reach], e_sc[reach, cols], ((1,), (0,)))
        total = acc[d : d + 1]
        acc = acc[:d]

        def forward(t, total):
            e = jnp.exp2(sp_sc[t] * EXP_SCALE - shift)
            small = e.astype(BF16)
            ep_sc[t] = small
            accp_sc[...] += dot(vtp_sc[t], small, ((1,), (0,)))
            return total + jnp.sum(e, axis=0, keepdims=True)

        if prev:
            accp_sc[...] = acc
            total = lax.fori_loop(first, prev_tiles, forward, total)
            acc = accp_sc[...]
        inverse = 1.0 / total
        attended = (acc * inverse).astype(BF16)
        gt = g.T.astype(F32)
        delta = jnp.sum(attended.astype(F32) * gt, axis=0, keepdims=True)
        gs_sc[:, cols] = (gt * inverse).astype(BF16)
        qs_sc[:, cols] = (q.T.astype(F32) * (inverse * ATTN_SCALE)).astype(BF16)

        for t in range(i + 1):
            at = slice(t * TILE, (t + 1) * TILE)
            dp = dot(x_ref[at, value_at : value_at + d], g, ((1,), (1,)))
            ds_sc[at, cols] = e_sc[at, cols] * (dp - delta).astype(BF16)
        dq = dot(kt_sc[:, reach], ds_sc[reach, cols], ((1,), (0,)))

        def backward(t, carry):
            e = ep_sc[t]
            dp = dot(vp_sc[t], g, ((1,), (1,)))
            ds = e * (dp - delta).astype(BF16)
            dkp_sc[t] += dot(qs_sc[:, cols], ds, ((1,), (1,)))
            dvp_sc[t] += dot(gs_sc[:, cols], e, ((1,), (1,)))
            dqp_sc[...] += dot(ktp_sc[t], ds, ((1,), (0,)))
            return carry

        if prev:
            dqp_sc[...] = dq
            lax.fori_loop(first, prev_tiles, backward, 0)
            dq = dqp_sc[...]
        attended = attended.T
        dq = (dq * (inverse * ATTN_SCALE)).astype(BF16).T
        for n in range(PER_GROUP):
            out_ref[span, n * d : (n + 1) * d] = attended[n * TILE : (n + 1) * TILE]
            out_ref[span, qw + n * d : qw + (n + 1) * d] = dq[n * TILE : (n + 1) * TILE]

    for t in range(q_tiles):
        at = slice(t * TILE, (t + 1) * TILE)
        collect(q_tiles - 1, t)
        dk = dkt_sc[:, at].T
        dv = dvt_sc[:, at].T
        if split:
            own_ref[at, 0:d] = dk
            own_ref[at, d : 2 * d] = dv
        else:
            out_ref[at, key_at : key_at + d] = dk.astype(BF16)
            out_ref[at, value_at : value_at + d] = dv.astype(BF16)
    for t in range(prev_tiles):
        back_ref[t * TILE : (t + 1) * TILE, 0:d] = dkp_sc[t].T.astype(BF16)
        back_ref[t * TILE : (t + 1) * TILE, d : 2 * d] = dvp_sc[t].T.astype(BF16)


def assemble(parts, subs, sub):
    rows = [None] * len(parts)
    for n, part in enumerate(parts):
        turn, base = n % subs, len(parts) - subs if n < subs else 0
        for p in range(subs):
            seen = rows[base + p]
            rows[base + p] = part if seen is None else jnp.where((sub ^ turn) == p, part, seen)
    return jnp.concatenate(rows, 0)


def decide_kernel(subs, run, blocks, place_ref, *refs):
    count = subs * (2 if blocks > 1 else 1)
    ids_ref, bounds_ref, needed_ref = refs[count:]
    block, sub = place_ref[0], place_ref[1]
    ahead = count - subs
    ids = assemble([ref[...] for ref in refs[:count]], subs, sub).astype(F32)
    ids_ref[...] = ids
    heads = jnp.min(ids, axis=1, keepdims=True)
    tails = jnp.max(ids, axis=1, keepdims=True)
    row = lax.broadcasted_iota(jnp.int32, (count, 1), 0)
    if ahead:
        after = jnp.sum((tails[ahead:] == heads[0:1]).astype(F32))
        needed = jnp.sum((tails[:ahead] == heads[ahead : ahead + 1]).astype(F32))
        if blocks > 2:
            after = 0.0
        needed_ref[0] = jnp.where(block == 0, after, needed).astype(jnp.int32)
        absent = (row < ahead) & (block == 0)
        heads = jnp.where(absent, -1.0, heads)
        tails = jnp.where(absent, -1.0, tails)
    else:
        needed_ref[0] = 0
    reach = WINDOW // run
    for i in range(subs):
        first = jnp.sum((tails < heads[ahead + i : ahead + i + 1]).astype(F32)).astype(jnp.int32)
        middle = jnp.sum((heads < tails[ahead + i : ahead + i + 1]).astype(F32)).astype(jnp.int32)
        bounds_ref[i] = jnp.maximum(first - ahead, i - reach)
        bounds_ref[subs + i] = jnp.maximum(middle - ahead, i + 1 - reach)
    bounds_ref[2 * subs] = block


def lowest_keys(ids, subs, block):
    count, run = ids.shape
    ahead = count - subs
    lane = lax.broadcasted_iota(jnp.int32, (count, run), 1)
    row = lax.broadcasted_iota(jnp.int32, (count, run), 0)
    spot = ((row - ahead) * run + lane).astype(F32)
    turned = pltpu.roll(ids, 1, 1)
    lagged = jnp.concatenate([turned[:1], turned[: count - 1]], 0)
    before = jnp.where(lane == 0, lagged, turned)
    opens = (ids != before) | ((lane == 0) & ((row == 0) | ((row == ahead) & (block == 0))))
    far = -4.0 * run * count
    start = jnp.where(opens, spot, far)
    step = 1
    while step < run:
        start = jnp.maximum(start, jnp.where(lane >= step, pltpu.roll(start, step, 1), far))
        step *= 2
    ends = jnp.max(start, axis=1, keepdims=True)
    best = [jnp.full((1, 1), far, F32)]
    for p in range(count - 1):
        best.append(jnp.maximum(best[-1], ends[p : p + 1]))
    start = jnp.maximum(start, jnp.concatenate(best, 0))
    return jnp.maximum(start, spot - (WINDOW - 1))[ahead:].astype(jnp.int32)


def attend(bounds, ids, x, before):
    rows = x.shape[0]
    prev = 0 if before is None else before.shape[0]
    split = prev > 0
    d = HEAD_DIM
    qw = PER_GROUP * d
    wide = PER_GROUP * TILE
    span = PER_GROUP * rows
    tiles = prev // TILE
    own_scratch = [
        pltpu.VMEM((d, rows), BF16),
        pltpu.VMEM((d + 16, rows), BF16),
        pltpu.VMEM((rows, wide), F32),
        pltpu.VMEM((rows, span), BF16),
        pltpu.VMEM((rows, span), BF16),
        pltpu.VMEM((d, span), BF16),
        pltpu.VMEM((d, span), BF16),
        pltpu.VMEM((d, rows), F32),
        pltpu.VMEM((d, rows), F32),
    ]
    prev_scratch = [
        pltpu.VMEM((tiles, TILE, d), BF16),
        pltpu.VMEM((tiles, TILE, d), BF16),
        pltpu.VMEM((tiles, d, TILE), BF16),
        pltpu.VMEM((tiles, d, TILE), BF16),
        pltpu.VMEM((tiles, TILE, wide), F32),
        pltpu.VMEM((tiles, TILE, wide), BF16),
        pltpu.VMEM((tiles, d, TILE), F32),
        pltpu.VMEM((tiles, d, TILE), F32),
        pltpu.VMEM((d, wide), F32),
        pltpu.VMEM((d, wide), F32),
    ]
    if split:
        out_shape = (
            jax.ShapeDtypeStruct((rows, 2 * qw), BF16),
            jax.ShapeDtypeStruct((rows, 2 * d), F32),
            jax.ShapeDtypeStruct((prev, 2 * d), BF16),
        )
        operands = (bounds, ids, x, before)
    else:
        out_shape = (jax.ShapeDtypeStruct((rows, 2 * qw + 2 * d), BF16),)
        operands = (bounds, ids, x)

    def kernel(*refs):
        attention_kernel(rows, prev, split, *refs)

    return pl.pallas_call(
        kernel,
        out_shape=out_shape,
        in_specs=[SCALARS] + [WHOLE] * (len(operands) - 1),
        out_specs=[WHOLE] * len(out_shape),
        scratch_shapes=own_scratch + (prev_scratch if split else []),
        compiler_params=pltpu.CompilerParams(vmem_limit_bytes=40 << 20),
    )(*operands)


def body(queries, keys, values, grad_out, segments):
    d = HEAD_DIM
    qw = PER_GROUP * d
    blocks, subs, heads = (lax.axis_size(a) for a in ("block", "sub", "head"))
    groups = subs * heads
    local = queries.shape[0]
    run = segments.shape[0]
    rows = run * subs
    assert groups == KVHEADS and rows == WINDOW and run == TILE

    packed = pl.pallas_call(
        lambda *refs: pack_kernel(groups, *refs),
        name="pack",
        out_shape=jax.ShapeDtypeStruct((groups, local, 2 * qw + 2 * d), BF16),
        in_specs=[ANYWHERE] * 4,
        out_specs=ANYWHERE,
        scratch_shapes=[
            pltpu.VMEM(queries.shape, BF16),
            pltpu.VMEM(queries.shape, BF16),
            pltpu.VMEM(keys.shape, BF16),
            pltpu.VMEM(keys.shape, BF16),
            pltpu.VMEM((groups, local, 2 * qw + 2 * d), BF16),
            pltpu.SemaphoreType.DMA((2, 4)),
            pltpu.SemaphoreType.DMA((groups,)),
        ],
    )(queries, grad_out, keys, values)
    x = lax.all_to_all(packed, ("sub", "head"), 0, 0, tiled=True).reshape(rows, 2 * qw + 2 * d)

    block = lax.axis_index("block")
    sub = lax.axis_index("sub")
    both = ("block", "sub")
    line = segments.reshape(1, run)

    def turned_ids(back):
        parts = []
        for turn in range(subs):
            route = [
                (((b - back) % blocks) * subs + (s ^ turn), b * subs + s)
                for b in range(blocks)
                for s in range(subs)
            ]
            parts.append(lax.ppermute(line, both, route) if back or turn else line)
        return parts

    parts = turned_ids(0) + (turned_ids(1) if blocks > 1 else [])
    ids, bounds, needed = pl.pallas_call(
        lambda *refs: decide_kernel(subs, run, blocks, *refs),
        name="decide",
        out_shape=(
            jax.ShapeDtypeStruct((len(parts), run), F32),
            jax.ShapeDtypeStruct((2 * subs + 1,), jnp.int32),
            jax.ShapeDtypeStruct((1,), jnp.int32),
        ),
        in_specs=[SCALARS] + [WHOLE] * len(parts),
        out_specs=[WHOLE, SCALARS, SCALARS],
        compiler_params=pltpu.CompilerParams(vmem_limit_bytes=1 << 20),
    )(jnp.stack([block, sub]), *parts)
    needed = needed.reshape(())
    if blocks > 2:
        step = 1
        while step < blocks:
            turned = lax.ppermute(needed, "block", [(i, (i + step) % blocks) for i in range(blocks)])
            needed = jnp.maximum(needed, turned)
            step *= 2

    def swap(value):
        return lax.all_to_all(value, ("sub", "head"), 0, 0, tiled=True)

    def unpack(*parts):
        return pl.pallas_call(
            lambda *refs: unpack_kernel(groups, len(parts), *refs),
            name="unpack",
            out_shape=(
                jax.ShapeDtypeStruct(queries.shape, BF16),
                jax.ShapeDtypeStruct(queries.shape, BF16),
                jax.ShapeDtypeStruct(keys.shape, BF16),
                jax.ShapeDtypeStruct(keys.shape, BF16),
            ),
            in_specs=[WHOLE] * len(parts),
            out_specs=[WHOLE] * 4,
            compiler_params=pltpu.CompilerParams(vmem_limit_bytes=8 << 20),
        )(*parts)

    def alone(x, ids, bounds):
        (out,) = attend(bounds, ids, x, None)
        return unpack(swap(out.reshape(groups, local, 2 * qw + 2 * d)))

    onward = [(i, i + 1) for i in range(blocks - 1)]
    backward = [(i + 1, i) for i in range(blocks - 1)]

    def fetch(count):
        def branch(x):
            tail = x[rows - count * run :, 2 * qw :]
            return jnp.pad(lax.ppermute(tail, "block", onward), ((rows - count * run, 0), (0, 0)))

        return branch

    def give(count):
        at = rows - count * run

        def branch(out, kv, back):
            late = lax.ppermute(back[at:], "block", backward)
            kv = (kv + jnp.pad(late.astype(F32), ((at, 0), (0, 0)))).astype(BF16)
            if 2 * count <= TOGETHER:
                both = jnp.concatenate([out, kv], 1)
                return unpack(swap(both.reshape(groups, local, 2 * qw + 2 * d)))
            main = swap(out.reshape(groups, local, 2 * qw))
            side = swap(kv.reshape(groups, local, 2 * d))
            return unpack(main, side)

        return branch

    def reaching(x, ids, bounds):
        case = jnp.clip(needed - 1, 0, subs - 1)
        before = lax.switch(case, [fetch(c + 1) for c in range(subs)], x)
        out, kv, back = attend(bounds, ids, x, before)
        return lax.switch(case, [give(c + 1) for c in range(subs)], out, kv, back)

    if blocks == 1:
        return alone(x, ids, bounds)
    return lax.cond(needed == 0, alone, reaching, x, ids, bounds)


def solution(mesh):
    shape = dict(mesh.shape)
    devices = np.asarray(mesh.devices)

    def program(queries, keys, values, grad_out, segments):
        run = segments.shape[0] // shape["ctx"]
        subs = WINDOW // run
        fine = Mesh(
            devices.reshape(shape["ctx"] // subs, subs, shape["head"]), ("block", "sub", "head")
        )
        spread = P(("block", "sub", "head"), None)
        return jax.shard_map(
            body,
            mesh=fine,
            in_specs=(spread, spread, spread, spread, P(("block", "sub"))),
            out_specs=(spread, spread, spread, spread),
            check_vma=False,
        )(queries, keys, values, grad_out, segments)

    return program
```

```python
import jax
import jax.numpy as jnp
import numpy as np
from jax import lax
from jax.experimental import pallas as pl
from jax.experimental.pallas import tpu as pltpu
from jax.sharding import Mesh, PartitionSpec as P


QHEADS = 32
KVHEADS = 16
HEAD_DIM = 128
WINDOW = 1024
PER_GROUP = QHEADS // KVHEADS

ATTN_SCALE = 168.0 ** (-0.5)
EXP_SCALE = ATTN_SCALE * 1.4426950408889634
HIDDEN = -1e30
TOGETHER = 2
SPLITS = 4
TILE = 256
F32 = jnp.float32
BF16 = jnp.bfloat16
WHOLE = pl.BlockSpec(memory_space=pltpu.VMEM)
ANYWHERE = pl.BlockSpec(memory_space=pl.ANY)
SCALARS = pl.BlockSpec(memory_space=pltpu.SMEM)


def dot(a, b, contract):
    return lax.dot_general(a, b, ((contract[0], contract[1]), ((), ())), preferred_element_type=F32)


def pack_kernel(groups, q_ref, g_ref, k_ref, v_ref, out_ref, q_sc, g_sc, k_sc, v_sc, hold, in_sem, out_sem):
    qw = PER_GROUP * HEAD_DIM
    kw = HEAD_DIM
    half = groups // SPLITS
    pairs = ((q_ref, q_sc, qw, 0), (g_ref, g_sc, qw, qw), (k_ref, k_sc, kw, 2 * qw), (v_ref, v_sc, kw, 2 * qw + kw))

    def fetch(part):
        return [
            pltpu.make_async_copy(
                ref.at[:, part * half * w : (part + 1) * half * w],
                sc.at[:, part * half * w : (part + 1) * half * w],
                in_sem.at[part, n],
            )
            for n, (ref, sc, w, at) in enumerate(pairs)
        ]

    def emit(j):
        return pltpu.make_async_copy(hold.at[j], out_ref.at[j], out_sem.at[j])

    for part in range(SPLITS):
        for copy in fetch(part):
            copy.start()
    for part in range(SPLITS):
        for copy in fetch(part):
            copy.wait()
        for j in range(part * half, (part + 1) * half):
            for ref, sc, w, at in pairs:
                hold[j, :, at : at + w] = sc[:, j * w : (j + 1) * w]
            emit(j).start()
    for j in range(groups):
        emit(j).wait()


def unpack_kernel(groups, count, *refs):
    ins, (o_ref, dq_ref, dk_ref, dv_ref) = refs[:count], refs[count:]
    main, side = ins[0], ins[-1]
    qw = PER_GROUP * HEAD_DIM
    kw = HEAD_DIM
    base = 2 * qw if count == 1 else 0
    for j in range(groups):
        o_ref[:, j * qw : (j + 1) * qw] = main[j, :, 0:qw]
        dq_ref[:, j * qw : (j + 1) * qw] = main[j, :, qw : 2 * qw]
        dk_ref[:, j * kw : (j + 1) * kw] = side[j, :, base : base + kw]
        dv_ref[:, j * kw : (j + 1) * kw] = side[j, :, base + kw : base + 2 * kw]


def attention_kernel(rows, prev, split, *refs):
    if prev:
        bounds_ref, ids_ref, x_ref, before_ref, *rest = refs
    else:
        bounds_ref, ids_ref, x_ref, *rest = refs
        before_ref = None
    if split:
        out_ref, own_ref, back_ref, *scratch = rest
        kp_sc, vp_sc, ktp_sc, vtp_sc, sp_sc, ep_sc, dkp_sc, dvp_sc, accp_sc, dqp_sc = scratch[9:]
    else:
        out_ref, *scratch = rest
        own_ref = back_ref = None
    kt_sc, vt_sc, s_sc, e_sc, ds_sc, qs_sc, gs_sc, dkt_sc, dvt_sc = scratch[:9]
    d = HEAD_DIM
    qw = PER_GROUP * d
    q_tiles = rows // TILE
    prev_tiles = prev // TILE
    wide = PER_GROUP * TILE
    key_at, value_at = 2 * qw, 2 * qw + d

    low_all = lowest_keys(ids_ref[...], q_tiles, bounds_ref[2 * q_tiles])
    lanes = lax.broadcasted_iota(jnp.int32, (1, wide), 1) % TILE
    key_rows = lax.broadcasted_iota(jnp.int32, (TILE, wide), 0)
    for t in range(prev_tiles):
        span = slice(t * TILE, (t + 1) * TILE)
        k, v = before_ref[span, 0:d], before_ref[span, d : 2 * d]
        kp_sc[t], vp_sc[t], ktp_sc[t], vtp_sc[t] = k, v, k.T, v.T
        dkp_sc[t] = jnp.zeros((d, TILE), F32)
        dvp_sc[t] = jnp.zeros((d, TILE), F32)

    def collect(i, t):
        at = slice(t * TILE, (t + 1) * TILE)
        cols = slice(i * wide, (i + 1) * wide)
        dk = dot(qs_sc[:, cols], ds_sc[at, cols], ((1,), (1,)))
        dv = dot(gs_sc[:, cols], e_sc[at, cols], ((1,), (1,)))
        if t == i:
            dkt_sc[:, at] = dk
            dvt_sc[:, at] = dv
        else:
            dkt_sc[:, at] += dk
            dvt_sc[:, at] += dv

    def own_scores(i, t, held):
        at = slice(t * TILE, (t + 1) * TILE)
        span = slice(i * TILE, (i + 1) * TILE)
        q = jnp.concatenate([x_ref[span, n * d : (n + 1) * d] for n in range(PER_GROUP)], 0)
        low = jnp.concatenate([low_all[i : i + 1]] * PER_GROUP, 1)
        s = dot(x_ref[at, key_at : key_at + d], q, ((1,), (1,)))
        s = jnp.where(key_rows >= low - t * TILE, s, HIDDEN)
        if t == i:
            s = jnp.where(key_rows <= lanes, s, HIDDEN)
        s_sc[i % 2, at, :] = s
        held[0] = jnp.maximum(held[0], jnp.max(s, axis=0, keepdims=True))

    ahead = None
    for i in range(q_tiles):
        span = slice(i * TILE, (i + 1) * TILE)
        cols = slice(i * wide, (i + 1) * wide)
        reach = slice(0, (i + 1) * TILE)
        kt_sc[:, span] = x_ref[span, key_at : key_at + d].T
        vt_sc[0:d, span] = x_ref[span, value_at : value_at + d].T
        vt_sc[d:, span] = jnp.ones((16, TILE), BF16)
        q = jnp.concatenate([x_ref[span, n * d : (n + 1) * d] for n in range(PER_GROUP)], 0)
        g = jnp.concatenate([x_ref[span, qw + n * d : qw + (n + 1) * d] for n in range(PER_GROUP)], 0)
        low = jnp.concatenate([low_all[i : i + 1]] * PER_GROUP, 1)
        first = jnp.maximum(bounds_ref[i] + prev_tiles, 0)

        if i == 0 or prev:
            ahead = [jnp.full((1, wide), HIDDEN, F32)]
            for t in range(i + 1):
                own_scores(i, t, ahead)
        top = ahead[0]

        def scores(t, top):
            s = dot(kp_sc[t], q, ((1,), (1,)))
            s = jnp.where(key_rows >= low - (t - prev_tiles) * TILE, s, HIDDEN)
            sp_sc[t] = s
            return jnp.maximum(top, jnp.max(s, axis=0, keepdims=True))

        if prev:
            top = lax.fori_loop(first, prev_tiles, scores, top)
        shift = top * EXP_SCALE

        for t in range(i + 1):
            at = slice(t * TILE, (t + 1) * TILE)
            e = jnp.exp2(s_sc[i % 2, at, :] * EXP_SCALE - shift)
            e_sc[at, cols] = e.astype(BF16)
            if t < i:
                collect(i - 1, t)
        acc = dot(vt_sc[:, reach], e_sc[reach, cols], ((1,), (0,)))
        total = acc[d : d + 1]
        acc = acc[:d]

        def forward(t, total):
            e = jnp.exp2(sp_sc[t] * EXP_SCALE - shift)
            small = e.astype(BF16)
            ep_sc[t] = small
            accp_sc[...] += dot(vtp_sc[t], small, ((1,), (0,)))
            return total + jnp.sum(e, axis=0, keepdims=True)

        if prev:
            accp_sc[...] = acc
            total = lax.fori_loop(first, prev_tiles, forward, total)
            acc = accp_sc[...]
        inverse = 1.0 / total
        attended = (acc * inverse).astype(BF16)
        gt = g.T.astype(F32)
        delta = jnp.sum(attended.astype(F32) * gt, axis=0, keepdims=True)
        gs_sc[:, cols] = (gt * inverse).astype(BF16)
        qs_sc[:, cols] = (q.T.astype(F32) * (inverse * ATTN_SCALE)).astype(BF16)

        held = [jnp.full((1, wide), HIDDEN, F32)]
        for t in range(i + 1):
            at = slice(t * TILE, (t + 1) * TILE)
            dp = dot(x_ref[at, value_at : value_at + d], g, ((1,), (1,)))
            ds_sc[at, cols] = e_sc[at, cols] * (dp - delta).astype(BF16)
            if not prev and i + 1 < q_tiles:
                own_scores(i + 1, t, held)
        if not prev and i + 1 < q_tiles:
            own_scores(i + 1, i + 1, held)
            ahead = held
        dq = dot(kt_sc[:, reach], ds_sc[reach, cols], ((1,), (0,)))

        def backward(t, carry):
            e = ep_sc[t]
            dp = dot(vp_sc[t], g, ((1,), (1,)))
            ds = e * (dp - delta).astype(BF16)
            dkp_sc[t] += dot(qs_sc[:, cols], ds, ((1,), (1,)))
            dvp_sc[t] += dot(gs_sc[:, cols], e, ((1,), (1,)))
            dqp_sc[...] += dot(ktp_sc[t], ds, ((1,), (0,)))
            return carry

        if prev:
            dqp_sc[...] = dq
            lax.fori_loop(first, prev_tiles, backward, 0)
            dq = dqp_sc[...]
        attended = attended.T
        dq = (dq * (inverse * ATTN_SCALE)).astype(BF16).T
        for n in range(PER_GROUP):
            out_ref[span, n * d : (n + 1) * d] = attended[n * TILE : (n + 1) * TILE]
            out_ref[span, qw + n * d : qw + (n + 1) * d] = dq[n * TILE : (n + 1) * TILE]

    for t in range(q_tiles):
        at = slice(t * TILE, (t + 1) * TILE)
        collect(q_tiles - 1, t)
        dk = dkt_sc[:, at].T
        dv = dvt_sc[:, at].T
        if split:
            own_ref[at, 0:d] = dk
            own_ref[at, d : 2 * d] = dv
        else:
            out_ref[at, key_at : key_at + d] = dk.astype(BF16)
            out_ref[at, value_at : value_at + d] = dv.astype(BF16)
    for t in range(prev_tiles):
        back_ref[t * TILE : (t + 1) * TILE, 0:d] = dkp_sc[t].T.astype(BF16)
        back_ref[t * TILE : (t + 1) * TILE, d : 2 * d] = dvp_sc[t].T.astype(BF16)


def assemble(parts, subs, sub):
    rows = [None] * len(parts)
    for n, part in enumerate(parts):
        turn, base = n % subs, len(parts) - subs if n < subs else 0
        for p in range(subs):
            seen = rows[base + p]
            rows[base + p] = part if seen is None else jnp.where((sub ^ turn) == p, part, seen)
    return jnp.concatenate(rows, 0)


def decide_kernel(subs, run, blocks, place_ref, *refs):
    count = subs * (2 if blocks > 1 else 1)
    ids_ref, bounds_ref, needed_ref = refs[count:]
    block, sub = place_ref[0], place_ref[1]
    ahead = count - subs
    ids = assemble([ref[...] for ref in refs[:count]], subs, sub).astype(F32)
    ids_ref[...] = ids
    heads = jnp.min(ids, axis=1, keepdims=True)
    tails = jnp.max(ids, axis=1, keepdims=True)
    row = lax.broadcasted_iota(jnp.int32, (count, 1), 0)
    if ahead:
        after = jnp.sum((tails[ahead:] == heads[0:1]).astype(F32))
        needed = jnp.sum((tails[:ahead] == heads[ahead : ahead + 1]).astype(F32))
        if blocks > 2:
            after = 0.0
        needed_ref[0] = jnp.where(block == 0, after, needed).astype(jnp.int32)
        absent = (row < ahead) & (block == 0)
        heads = jnp.where(absent, -1.0, heads)
        tails = jnp.where(absent, -1.0, tails)
    else:
        needed_ref[0] = 0
    reach = WINDOW // run
    for i in range(subs):
        first = jnp.sum((tails < heads[ahead + i : ahead + i + 1]).astype(F32)).astype(jnp.int32)
        middle = jnp.sum((heads < tails[ahead + i : ahead + i + 1]).astype(F32)).astype(jnp.int32)
        bounds_ref[i] = jnp.maximum(first - ahead, i - reach)
        bounds_ref[subs + i] = jnp.maximum(middle - ahead, i + 1 - reach)
    bounds_ref[2 * subs] = block


def lowest_keys(ids, subs, block):
    count, run = ids.shape
    ahead = count - subs
    lane = lax.broadcasted_iota(jnp.int32, (count, run), 1)
    row = lax.broadcasted_iota(jnp.int32, (count, run), 0)
    spot = ((row - ahead) * run + lane).astype(F32)
    turned = pltpu.roll(ids, 1, 1)
    lagged = jnp.concatenate([turned[:1], turned[: count - 1]], 0)
    before = jnp.where(lane == 0, lagged, turned)
    opens = (ids != before) | ((lane == 0) & ((row == 0) | ((row == ahead) & (block == 0))))
    far = -4.0 * run * count
    start = jnp.where(opens, spot, far)
    step = 1
    while step < run:
        start = jnp.maximum(start, jnp.where(lane >= step, pltpu.roll(start, step, 1), far))
        step *= 2
    ends = jnp.max(start, axis=1, keepdims=True)
    best = [jnp.full((1, 1), far, F32)]
    for p in range(count - 1):
        best.append(jnp.maximum(best[-1], ends[p : p + 1]))
    start = jnp.maximum(start, jnp.concatenate(best, 0))
    return jnp.maximum(start, spot - (WINDOW - 1))[ahead:].astype(jnp.int32)


def attend(bounds, ids, x, before):
    rows = x.shape[0]
    prev = 0 if before is None else before.shape[0]
    split = prev > 0
    d = HEAD_DIM
    qw = PER_GROUP * d
    wide = PER_GROUP * TILE
    span = PER_GROUP * rows
    tiles = prev // TILE
    own_scratch = [
        pltpu.VMEM((d, rows), BF16),
        pltpu.VMEM((d + 16, rows), BF16),
        pltpu.VMEM((2, rows, wide), F32),
        pltpu.VMEM((rows, span), BF16),
        pltpu.VMEM((rows, span), BF16),
        pltpu.VMEM((d, span), BF16),
        pltpu.VMEM((d, span), BF16),
        pltpu.VMEM((d, rows), F32),
        pltpu.VMEM((d, rows), F32),
    ]
    prev_scratch = [
        pltpu.VMEM((tiles, TILE, d), BF16),
        pltpu.VMEM((tiles, TILE, d), BF16),
        pltpu.VMEM((tiles, d, TILE), BF16),
        pltpu.VMEM((tiles, d, TILE), BF16),
        pltpu.VMEM((tiles, TILE, wide), F32),
        pltpu.VMEM((tiles, TILE, wide), BF16),
        pltpu.VMEM((tiles, d, TILE), F32),
        pltpu.VMEM((tiles, d, TILE), F32),
        pltpu.VMEM((d, wide), F32),
        pltpu.VMEM((d, wide), F32),
    ]
    if split:
        out_shape = (
            jax.ShapeDtypeStruct((rows, 2 * qw), BF16),
            jax.ShapeDtypeStruct((rows, 2 * d), F32),
            jax.ShapeDtypeStruct((prev, 2 * d), BF16),
        )
        operands = (bounds, ids, x, before)
    else:
        out_shape = (jax.ShapeDtypeStruct((rows, 2 * qw + 2 * d), BF16),)
        operands = (bounds, ids, x)

    def kernel(*refs):
        attention_kernel(rows, prev, split, *refs)

    return pl.pallas_call(
        kernel,
        out_shape=out_shape,
        in_specs=[SCALARS] + [WHOLE] * (len(operands) - 1),
        out_specs=[WHOLE] * len(out_shape),
        scratch_shapes=own_scratch + (prev_scratch if split else []),
        compiler_params=pltpu.CompilerParams(vmem_limit_bytes=40 << 20),
    )(*operands)


def body(queries, keys, values, grad_out, segments):
    d = HEAD_DIM
    qw = PER_GROUP * d
    blocks, subs, heads = (lax.axis_size(a) for a in ("block", "sub", "head"))
    groups = subs * heads
    local = queries.shape[0]
    run = segments.shape[0]
    rows = run * subs
    assert groups == KVHEADS and rows == WINDOW and run == TILE

    packed = pl.pallas_call(
        lambda *refs: pack_kernel(groups, *refs),
        name="pack",
        out_shape=jax.ShapeDtypeStruct((groups, local, 2 * qw + 2 * d), BF16),
        in_specs=[ANYWHERE] * 4,
        out_specs=ANYWHERE,
        scratch_shapes=[
            pltpu.VMEM(queries.shape, BF16),
            pltpu.VMEM(queries.shape, BF16),
            pltpu.VMEM(keys.shape, BF16),
            pltpu.VMEM(keys.shape, BF16),
            pltpu.VMEM((groups, local, 2 * qw + 2 * d), BF16),
            pltpu.SemaphoreType.DMA((SPLITS, 4)),
            pltpu.SemaphoreType.DMA((groups,)),
        ],
    )(queries, grad_out, keys, values)
    x = lax.all_to_all(packed, ("sub", "head"), 0, 0, tiled=True).reshape(rows, 2 * qw + 2 * d)

    block = lax.axis_index("block")
    sub = lax.axis_index("sub")
    both = ("block", "sub")
    line = segments.reshape(1, run)

    def turned_ids(back):
        parts = []
        for turn in range(subs):
            route = [
                (((b - back) % blocks) * subs + (s ^ turn), b * subs + s)
                for b in range(blocks)
                for s in range(subs)
                if b or not back or s == turn
            ]
            parts.append(lax.ppermute(line, both, route) if back or turn else line)
        return parts

    parts = turned_ids(0) + (turned_ids(1) if blocks > 1 else [])
    ids, bounds, needed = pl.pallas_call(
        lambda *refs: decide_kernel(subs, run, blocks, *refs),
        name="decide",
        out_shape=(
            jax.ShapeDtypeStruct((len(parts), run), F32),
            jax.ShapeDtypeStruct((2 * subs + 1,), jnp.int32),
            jax.ShapeDtypeStruct((1,), jnp.int32),
        ),
        in_specs=[SCALARS] + [WHOLE] * len(parts),
        out_specs=[WHOLE, SCALARS, SCALARS],
        compiler_params=pltpu.CompilerParams(vmem_limit_bytes=1 << 20),
    )(jnp.stack([block, sub]), *parts)
    needed = needed.reshape(())
    if blocks > 2:
        step = 1
        while step < blocks:
            turned = lax.ppermute(needed, "block", [(i, (i + step) % blocks) for i in range(blocks)])
            needed = jnp.maximum(needed, turned)
            step *= 2

    def swap(value):
        return lax.all_to_all(value, ("sub", "head"), 0, 0, tiled=True)

    def unpack(*parts):
        return pl.pallas_call(
            lambda *refs: unpack_kernel(groups, len(parts), *refs),
            name="unpack",
            out_shape=(
                jax.ShapeDtypeStruct(queries.shape, BF16),
                jax.ShapeDtypeStruct(queries.shape, BF16),
                jax.ShapeDtypeStruct(keys.shape, BF16),
                jax.ShapeDtypeStruct(keys.shape, BF16),
            ),
            in_specs=[WHOLE] * len(parts),
            out_specs=[WHOLE] * 4,
            compiler_params=pltpu.CompilerParams(vmem_limit_bytes=8 << 20),
        )(*parts)

    def alone(x, ids, bounds):
        (out,) = attend(bounds, ids, x, None)
        return unpack(swap(out.reshape(groups, local, 2 * qw + 2 * d)))

    onward = [(i, i + 1) for i in range(blocks - 1)]
    backward = [(i + 1, i) for i in range(blocks - 1)]

    def fetch(count):
        def branch(x):
            tail = x[rows - count * run :, 2 * qw :]
            return jnp.pad(lax.ppermute(tail, "block", onward), ((rows - count * run, 0), (0, 0)))

        return branch

    def give(count):
        at = rows - count * run

        def branch(out, kv, back):
            late = lax.ppermute(back[at:], "block", backward)
            kv = (kv + jnp.pad(late.astype(F32), ((at, 0), (0, 0)))).astype(BF16)
            if 2 * count <= TOGETHER:
                both = jnp.concatenate([out, kv], 1)
                return unpack(swap(both.reshape(groups, local, 2 * qw + 2 * d)))
            main = swap(out.reshape(groups, local, 2 * qw))
            side = swap(kv.reshape(groups, local, 2 * d))
            return unpack(main, side)

        return branch

    def reaching(x, ids, bounds):
        case = jnp.clip(needed - 1, 0, subs - 1)
        before = lax.switch(case, [fetch(c + 1) for c in range(subs)], x)
        out, kv, back = attend(bounds, ids, x, before)
        return lax.switch(case, [give(c + 1) for c in range(subs)], out, kv, back)

    if blocks == 1:
        return alone(x, ids, bounds)
    return lax.cond(needed == 0, alone, reaching, x, ids, bounds)


def solution(mesh):
    shape = dict(mesh.shape)
    devices = np.asarray(mesh.devices)

    def program(queries, keys, values, grad_out, segments):
        run = segments.shape[0] // shape["ctx"]
        subs = WINDOW // run
        fine = Mesh(
            devices.reshape(shape["ctx"] // subs, subs, shape["head"]), ("block", "sub", "head")
        )
        spread = P(("block", "sub", "head"), None)
        return jax.shard_map(
            body,
            mesh=fine,
            in_specs=(spread, spread, spread, spread, P(("block", "sub"))),
            out_specs=(spread, spread, spread, spread),
            check_vma=False,
        )(queries, keys, values, grad_out, segments)

    return program
```

```python
import jax
import jax.numpy as jnp
import numpy as np
from jax import lax
from jax.experimental import pallas as pl
from jax.experimental.pallas import tpu as pltpu
from jax.sharding import Mesh, PartitionSpec as P


QHEADS = 32
KVHEADS = 16
HEAD_DIM = 128
WINDOW = 1024
PER_GROUP = QHEADS // KVHEADS

ATTN_SCALE = 168.0 ** (-0.5)
EXP_SCALE = ATTN_SCALE * 1.4426950408889634
HIDDEN = -1e30
TOGETHER = 2
SPLITS = 4
TILE = 256
F32 = jnp.float32
BF16 = jnp.bfloat16
WHOLE = pl.BlockSpec(memory_space=pltpu.VMEM)
ANYWHERE = pl.BlockSpec(memory_space=pl.ANY)
SCALARS = pl.BlockSpec(memory_space=pltpu.SMEM)


def dot(a, b, contract):
    return lax.dot_general(a, b, ((contract[0], contract[1]), ((), ())), preferred_element_type=F32)


def pack_kernel(groups, q_ref, g_ref, k_ref, v_ref, out_ref, q_sc, g_sc, k_sc, v_sc, hold, in_sem, out_sem):
    qw = PER_GROUP * HEAD_DIM
    kw = HEAD_DIM
    half = groups // SPLITS
    pairs = ((q_ref, q_sc, qw, 0), (g_ref, g_sc, qw, qw), (k_ref, k_sc, kw, 2 * qw), (v_ref, v_sc, kw, 2 * qw + kw))

    def fetch(part):
        return [
            pltpu.make_async_copy(
                ref.at[:, part * half * w : (part + 1) * half * w],
                sc.at[:, part * half * w : (part + 1) * half * w],
                in_sem.at[part, n],
            )
            for n, (ref, sc, w, at) in enumerate(pairs)
        ]

    def emit(j):
        return pltpu.make_async_copy(hold.at[j], out_ref.at[j], out_sem.at[j])

    for part in range(SPLITS):
        for copy in fetch(part):
            copy.start()
    for part in range(SPLITS):
        for copy in fetch(part):
            copy.wait()
        for j in range(part * half, (part + 1) * half):
            for ref, sc, w, at in pairs:
                hold[j, :, at : at + w] = sc[:, j * w : (j + 1) * w]
            emit(j).start()
    for j in range(groups):
        emit(j).wait()


def unpack_kernel(groups, count, *refs):
    ins, (o_ref, dq_ref, dk_ref, dv_ref) = refs[:count], refs[count:]
    main, side = ins[0], ins[-1]
    qw = PER_GROUP * HEAD_DIM
    kw = HEAD_DIM
    base = 2 * qw if count == 1 else 0
    for j in range(groups):
        o_ref[:, j * qw : (j + 1) * qw] = main[j, :, 0:qw]
        dq_ref[:, j * qw : (j + 1) * qw] = main[j, :, qw : 2 * qw]
        dk_ref[:, j * kw : (j + 1) * kw] = side[j, :, base : base + kw]
        dv_ref[:, j * kw : (j + 1) * kw] = side[j, :, base + kw : base + 2 * kw]


def attention_kernel(rows, prev, split, *refs):
    if prev:
        place_ref, ids_ref, x_ref, before_ref, *rest = refs
    else:
        place_ref, ids_ref, x_ref, *rest = refs
        before_ref = None
    if split:
        out_ref, own_ref, back_ref, *scratch = rest
        kp_sc, vp_sc, ktp_sc, vtp_sc, sp_sc, ep_sc, dkp_sc, dvp_sc, accp_sc, dqp_sc = scratch[9:]
    else:
        out_ref, *scratch = rest
        own_ref = back_ref = None
    kt_sc, vt_sc, s_sc, e_sc, ds_sc, qs_sc, gs_sc, dkt_sc, dvt_sc = scratch[:9]
    d = HEAD_DIM
    qw = PER_GROUP * d
    q_tiles = rows // TILE
    prev_tiles = prev // TILE
    wide = PER_GROUP * TILE
    key_at, value_at = 2 * qw, 2 * qw + d

    low_all = lowest_keys(ids_ref[...], q_tiles, place_ref[0])
    firsts = first_tiles(ids_ref[...], q_tiles, place_ref[0]) if prev else None
    lanes = lax.broadcasted_iota(jnp.int32, (1, wide), 1) % TILE
    key_rows = lax.broadcasted_iota(jnp.int32, (TILE, wide), 0)
    for t in range(prev_tiles):
        span = slice(t * TILE, (t + 1) * TILE)

        @pl.when(t - prev_tiles >= firsts[0])
        def _():
            k, v = before_ref[span, 0:d], before_ref[span, d : 2 * d]
            kp_sc[t], vp_sc[t], ktp_sc[t], vtp_sc[t] = k, v, k.T, v.T

        dkp_sc[t] = jnp.zeros((d, TILE), F32)
        dvp_sc[t] = jnp.zeros((d, TILE), F32)

    def collect(i, t):
        at = slice(t * TILE, (t + 1) * TILE)
        cols = slice(i * wide, (i + 1) * wide)
        dk = dot(qs_sc[:, cols], ds_sc[at, cols], ((1,), (1,)))
        dv = dot(gs_sc[:, cols], e_sc[at, cols], ((1,), (1,)))
        if t == i:
            dkt_sc[:, at] = dk
            dvt_sc[:, at] = dv
        else:
            dkt_sc[:, at] += dk
            dvt_sc[:, at] += dv

    def own_scores(i, t, held):
        at = slice(t * TILE, (t + 1) * TILE)
        span = slice(i * TILE, (i + 1) * TILE)
        q = jnp.concatenate([x_ref[span, n * d : (n + 1) * d] for n in range(PER_GROUP)], 0)
        low = jnp.concatenate([low_all[i : i + 1]] * PER_GROUP, 1)
        s = dot(x_ref[at, key_at : key_at + d], q, ((1,), (1,)))
        s = jnp.where(key_rows >= low - t * TILE, s, HIDDEN)
        if t == i:
            s = jnp.where(key_rows <= lanes, s, HIDDEN)
        s_sc[i % 2, at, :] = s
        held[0] = jnp.maximum(held[0], jnp.max(s, axis=0, keepdims=True))

    ahead = None
    for i in range(q_tiles):
        span = slice(i * TILE, (i + 1) * TILE)
        cols = slice(i * wide, (i + 1) * wide)
        reach = slice(0, (i + 1) * TILE)
        kt_sc[:, span] = x_ref[span, key_at : key_at + d].T
        vt_sc[0:d, span] = x_ref[span, value_at : value_at + d].T
        vt_sc[d:, span] = jnp.ones((16, TILE), BF16)
        q = jnp.concatenate([x_ref[span, n * d : (n + 1) * d] for n in range(PER_GROUP)], 0)
        g = jnp.concatenate([x_ref[span, qw + n * d : qw + (n + 1) * d] for n in range(PER_GROUP)], 0)
        low = jnp.concatenate([low_all[i : i + 1]] * PER_GROUP, 1)
        first = jnp.maximum(firsts[i] + prev_tiles, 0) if prev else 0

        if i == 0 or prev:
            ahead = [jnp.full((1, wide), HIDDEN, F32)]
            for t in range(i + 1):
                own_scores(i, t, ahead)
        top = ahead[0]

        def scores(t, top):
            s = dot(kp_sc[t], q, ((1,), (1,)))
            s = jnp.where(key_rows >= low - (t - prev_tiles) * TILE, s, HIDDEN)
            sp_sc[t] = s
            return jnp.maximum(top, jnp.max(s, axis=0, keepdims=True))

        if prev:
            top = lax.fori_loop(first, prev_tiles, scores, top)
        shift = top * EXP_SCALE

        for t in range(i + 1):
            at = slice(t * TILE, (t + 1) * TILE)
            e = jnp.exp2(s_sc[i % 2, at, :] * EXP_SCALE - shift)
            e_sc[at, cols] = e.astype(BF16)
            if t < i:
                collect(i - 1, t)
        acc = dot(vt_sc[:, reach], e_sc[reach, cols], ((1,), (0,)))
        total = acc[d : d + 1]
        acc = acc[:d]

        def forward(t, total):
            e = jnp.exp2(sp_sc[t] * EXP_SCALE - shift)
            small = e.astype(BF16)
            ep_sc[t] = small
            accp_sc[...] += dot(vtp_sc[t], small, ((1,), (0,)))
            return total + jnp.sum(e, axis=0, keepdims=True)

        if prev:
            accp_sc[...] = acc
            total = lax.fori_loop(first, prev_tiles, forward, total)
            acc = accp_sc[...]
        inverse = 1.0 / total
        attended = (acc * inverse).astype(BF16)
        gt = g.T.astype(F32)
        delta = jnp.sum(attended.astype(F32) * gt, axis=0, keepdims=True)
        gs_sc[:, cols] = (gt * inverse).astype(BF16)
        qs_sc[:, cols] = (q.T.astype(F32) * (inverse * ATTN_SCALE)).astype(BF16)

        held = [jnp.full((1, wide), HIDDEN, F32)]
        for t in range(i + 1):
            at = slice(t * TILE, (t + 1) * TILE)
            dp = dot(x_ref[at, value_at : value_at + d], g, ((1,), (1,)))
            ds_sc[at, cols] = e_sc[at, cols] * (dp - delta).astype(BF16)
            if not prev and i + 1 < q_tiles:
                own_scores(i + 1, t, held)
        if not prev and i + 1 < q_tiles:
            own_scores(i + 1, i + 1, held)
            ahead = held
        dq = dot(kt_sc[:, reach], ds_sc[reach, cols], ((1,), (0,)))

        def backward(t, carry):
            e = ep_sc[t]
            dp = dot(vp_sc[t], g, ((1,), (1,)))
            ds = e * (dp - delta).astype(BF16)
            dkp_sc[t] += dot(qs_sc[:, cols], ds, ((1,), (1,)))
            dvp_sc[t] += dot(gs_sc[:, cols], e, ((1,), (1,)))
            dqp_sc[...] += dot(ktp_sc[t], ds, ((1,), (0,)))
            return carry

        if prev:
            dqp_sc[...] = dq
            lax.fori_loop(first, prev_tiles, backward, 0)
            dq = dqp_sc[...]
        attended = attended.T
        dq = (dq * (inverse * ATTN_SCALE)).astype(BF16).T
        for n in range(PER_GROUP):
            out_ref[span, n * d : (n + 1) * d] = attended[n * TILE : (n + 1) * TILE]
            out_ref[span, qw + n * d : qw + (n + 1) * d] = dq[n * TILE : (n + 1) * TILE]

    for t in range(q_tiles):
        at = slice(t * TILE, (t + 1) * TILE)
        collect(q_tiles - 1, t)
        dk = dkt_sc[:, at].T
        dv = dvt_sc[:, at].T
        if split:
            own_ref[at, 0:d] = dk
            own_ref[at, d : 2 * d] = dv
        else:
            out_ref[at, key_at : key_at + d] = dk.astype(BF16)
            out_ref[at, value_at : value_at + d] = dv.astype(BF16)
    for t in range(prev_tiles):
        back_ref[t * TILE : (t + 1) * TILE, 0:d] = dkp_sc[t].T.astype(BF16)
        back_ref[t * TILE : (t + 1) * TILE, d : 2 * d] = dvp_sc[t].T.astype(BF16)


def assemble(parts, subs, sub):
    rows = [None] * len(parts)
    for n, part in enumerate(parts):
        turn, base = n % subs, len(parts) - subs if n < subs else 0
        for p in range(subs):
            seen = rows[base + p]
            rows[base + p] = part if seen is None else jnp.where((sub ^ turn) == p, part, seen)
    return jnp.concatenate(rows, 0)


def decide_kernel(subs, blocks, place_ref, *refs):
    count = subs * (2 if blocks > 1 else 1)
    ids_ref, needed_ref = refs[count:]
    block, sub = place_ref[0], place_ref[1]
    ahead = count - subs
    ids = assemble([ref[...] for ref in refs[:count]], subs, sub).astype(F32)
    ids_ref[...] = ids
    heads = jnp.min(ids, axis=1, keepdims=True)
    tails = jnp.max(ids, axis=1, keepdims=True)
    if ahead:
        after = jnp.sum((tails[ahead:] == heads[0:1]).astype(F32))
        needed = jnp.sum((tails[:ahead] == heads[ahead : ahead + 1]).astype(F32))
        if blocks > 2:
            after = 0.0
        needed_ref[0] = jnp.where(block == 0, after, needed).astype(jnp.int32)
    else:
        needed_ref[0] = 0


def first_tiles(ids, subs, block):
    count, run = ids.shape
    ahead = count - subs
    row = lax.broadcasted_iota(jnp.int32, (count, 1), 0)
    heads = jnp.min(ids, axis=1, keepdims=True)
    tails = jnp.where((row < ahead) & (block == 0), -1.0, jnp.max(ids, axis=1, keepdims=True))
    firsts = []
    for i in range(subs):
        first = jnp.sum((tails < heads[ahead + i : ahead + i + 1]).astype(F32)).astype(jnp.int32)
        firsts.append(jnp.maximum(first - ahead, i - WINDOW // run))
    return firsts


def lowest_keys(ids, subs, block):
    count, run = ids.shape
    ahead = count - subs
    lane = lax.broadcasted_iota(jnp.int32, (count, run), 1)
    row = lax.broadcasted_iota(jnp.int32, (count, run), 0)
    spot = ((row - ahead) * run + lane).astype(F32)
    turned = pltpu.roll(ids, 1, 1)
    lagged = jnp.concatenate([turned[:1], turned[: count - 1]], 0)
    before = jnp.where(lane == 0, lagged, turned)
    opens = (ids != before) | ((lane == 0) & ((row == 0) | ((row == ahead) & (block == 0))))
    far = -4.0 * run * count
    start = jnp.where(opens, spot, far)
    step = 1
    while step < run:
        start = jnp.maximum(start, jnp.where(lane >= step, pltpu.roll(start, step, 1), far))
        step *= 2
    ends = jnp.max(start, axis=1, keepdims=True)
    best = [jnp.full((1, 1), far, F32)]
    for p in range(count - 1):
        best.append(jnp.maximum(best[-1], ends[p : p + 1]))
    start = jnp.maximum(start, jnp.concatenate(best, 0))
    return jnp.maximum(start, spot - (WINDOW - 1))[ahead:].astype(jnp.int32)


def attend(place, ids, x, before):
    rows = x.shape[0]
    prev = 0 if before is None else before.shape[0]
    split = prev > 0
    d = HEAD_DIM
    qw = PER_GROUP * d
    wide = PER_GROUP * TILE
    span = PER_GROUP * rows
    tiles = prev // TILE
    own_scratch = [
        pltpu.VMEM((d, rows), BF16),
        pltpu.VMEM((d + 16, rows), BF16),
        pltpu.VMEM((2, rows, wide), F32),
        pltpu.VMEM((rows, span), BF16),
        pltpu.VMEM((rows, span), BF16),
        pltpu.VMEM((d, span), BF16),
        pltpu.VMEM((d, span), BF16),
        pltpu.VMEM((d, rows), F32),
        pltpu.VMEM((d, rows), F32),
    ]
    prev_scratch = [
        pltpu.VMEM((tiles, TILE, d), BF16),
        pltpu.VMEM((tiles, TILE, d), BF16),
        pltpu.VMEM((tiles, d, TILE), BF16),
        pltpu.VMEM((tiles, d, TILE), BF16),
        pltpu.VMEM((tiles, TILE, wide), F32),
        pltpu.VMEM((tiles, TILE, wide), BF16),
        pltpu.VMEM((tiles, d, TILE), F32),
        pltpu.VMEM((tiles, d, TILE), F32),
        pltpu.VMEM((d, wide), F32),
        pltpu.VMEM((d, wide), F32),
    ]
    if split:
        out_shape = (
            jax.ShapeDtypeStruct((rows, 2 * qw), BF16),
            jax.ShapeDtypeStruct((rows, 2 * d), F32),
            jax.ShapeDtypeStruct((prev, 2 * d), BF16),
        )
        operands = (place, ids, x, before)
    else:
        out_shape = (jax.ShapeDtypeStruct((rows, 2 * qw + 2 * d), BF16),)
        operands = (place, ids, x)

    def kernel(*refs):
        attention_kernel(rows, prev, split, *refs)

    return pl.pallas_call(
        kernel,
        out_shape=out_shape,
        in_specs=[SCALARS] + [WHOLE] * (len(operands) - 1),
        out_specs=[WHOLE] * len(out_shape),
        scratch_shapes=own_scratch + (prev_scratch if split else []),
        compiler_params=pltpu.CompilerParams(vmem_limit_bytes=40 << 20),
    )(*operands)


def body(queries, keys, values, grad_out, segments):
    d = HEAD_DIM
    qw = PER_GROUP * d
    blocks, subs, heads = (lax.axis_size(a) for a in ("block", "sub", "head"))
    groups = subs * heads
    local = queries.shape[0]
    run = segments.shape[0]
    rows = run * subs
    assert groups == KVHEADS and rows == WINDOW and run == TILE

    packed = pl.pallas_call(
        lambda *refs: pack_kernel(groups, *refs),
        name="pack",
        out_shape=jax.ShapeDtypeStruct((groups, local, 2 * qw + 2 * d), BF16),
        in_specs=[ANYWHERE] * 4,
        out_specs=ANYWHERE,
        scratch_shapes=[
            pltpu.VMEM(queries.shape, BF16),
            pltpu.VMEM(queries.shape, BF16),
            pltpu.VMEM(keys.shape, BF16),
            pltpu.VMEM(keys.shape, BF16),
            pltpu.VMEM((groups, local, 2 * qw + 2 * d), BF16),
            pltpu.SemaphoreType.DMA((SPLITS, 4)),
            pltpu.SemaphoreType.DMA((groups,)),
        ],
    )(queries, grad_out, keys, values)
    x = lax.all_to_all(packed, ("sub", "head"), 0, 0, tiled=True).reshape(rows, 2 * qw + 2 * d)

    block = lax.axis_index("block")
    sub = lax.axis_index("sub")
    both = ("block", "sub")
    line = segments.reshape(1, run)

    def turned_ids(back):
        parts = []
        for turn in range(subs):
            route = [
                (((b - back) % blocks) * subs + (s ^ turn), b * subs + s)
                for b in range(blocks)
                for s in range(subs)
                if b or not back or s == turn
            ]
            parts.append(lax.ppermute(line, both, route) if back or turn else line)
        return parts

    parts = turned_ids(0) + (turned_ids(1) if blocks > 1 else [])
    place = jnp.stack([block, sub])
    ids, needed = pl.pallas_call(
        lambda *refs: decide_kernel(subs, blocks, *refs),
        name="decide",
        out_shape=(
            jax.ShapeDtypeStruct((len(parts), run), F32),
            jax.ShapeDtypeStruct((1,), jnp.int32),
        ),
        in_specs=[SCALARS] + [WHOLE] * len(parts),
        out_specs=[WHOLE, SCALARS],
        compiler_params=pltpu.CompilerParams(vmem_limit_bytes=1 << 20),
    )(place, *parts)
    needed = needed.reshape(())
    if blocks > 2:
        step = 1
        while step < blocks:
            turned = lax.ppermute(needed, "block", [(i, (i + step) % blocks) for i in range(blocks)])
            needed = jnp.maximum(needed, turned)
            step *= 2

    def swap(value):
        return lax.all_to_all(value, ("sub", "head"), 0, 0, tiled=True)

    def unpack(*parts):
        return pl.pallas_call(
            lambda *refs: unpack_kernel(groups, len(parts), *refs),
            name="unpack",
            out_shape=(
                jax.ShapeDtypeStruct(queries.shape, BF16),
                jax.ShapeDtypeStruct(queries.shape, BF16),
                jax.ShapeDtypeStruct(keys.shape, BF16),
                jax.ShapeDtypeStruct(keys.shape, BF16),
            ),
            in_specs=[WHOLE] * len(parts),
            out_specs=[WHOLE] * 4,
            compiler_params=pltpu.CompilerParams(vmem_limit_bytes=8 << 20),
        )(*parts)

    def alone(x, ids, place):
        (out,) = attend(place, ids, x, None)
        return unpack(swap(out.reshape(groups, local, 2 * qw + 2 * d)))

    onward = [(i, i + 1) for i in range(blocks - 1)]
    backward = [(i + 1, i) for i in range(blocks - 1)]

    def fetch(count):
        def branch(x):
            tail = x[rows - count * run :, 2 * qw :]
            return jnp.pad(lax.ppermute(tail, "block", onward), ((rows - count * run, 0), (0, 0)))

        return branch

    def give(count):
        at = rows - count * run

        def branch(out, kv, back):
            late = lax.ppermute(back[at:], "block", backward)
            kv = (kv + jnp.pad(late.astype(F32), ((at, 0), (0, 0)))).astype(BF16)
            if 2 * count <= TOGETHER:
                both = jnp.concatenate([out, kv], 1)
                return unpack(swap(both.reshape(groups, local, 2 * qw + 2 * d)))
            main = swap(out.reshape(groups, local, 2 * qw))
            side = swap(kv.reshape(groups, local, 2 * d))
            return unpack(main, side)

        return branch

    def reaching(x, ids, place):
        case = jnp.clip(needed - 1, 0, subs - 1)
        before = lax.switch(case, [fetch(c + 1) for c in range(subs)], x)
        out, kv, back = attend(place, ids, x, before)
        return lax.switch(case, [give(c + 1) for c in range(subs)], out, kv, back)

    if blocks == 1:
        return alone(x, ids, place)
    return lax.cond(needed == 0, alone, reaching, x, ids, place)


def solution(mesh):
    shape = dict(mesh.shape)
    devices = np.asarray(mesh.devices)

    def program(queries, keys, values, grad_out, segments):
        run = segments.shape[0] // shape["ctx"]
        subs = WINDOW // run
        fine = Mesh(
            devices.reshape(shape["ctx"] // subs, subs, shape["head"]), ("block", "sub", "head")
        )
        spread = P(("block", "sub", "head"), None)
        return jax.shard_map(
            body,
            mesh=fine,
            in_specs=(spread, spread, spread, spread, P(("block", "sub"))),
            out_specs=(spread, spread, spread, spread),
            check_vma=False,
        )(queries, keys, values, grad_out, segments)

    return program
```
